768 devices in a mesh: group: 12 (over z_hi, x), fsdp: 8 (over z_lo, core), tp: 8 (over y).
Axes of the slice: x: 4, y: 8, z: 12 (z_hi: 3, z_lo: 4; z = z_hi * 4 + z_lo), core: 2. Of those that a mesh axis runs over, the one named last changes fastest.
Arguments:
- tokens: bfloat16 [768, 4, 5120], P(('group', 'fsdp')), may hold values from -6 to 6
- queries: bfloat16 [768, 4, 5120], P(('group', 'fsdp'), None, 'tp'), may hold values from -6 to 6
- cache_keys: bfloat16 [768, 512, 1024], P(('group', 'fsdp'), None, 'tp'), may hold values from -6 to 6
- cache_values: bfloat16 [768, 512, 1024], P(('group', 'fsdp'), None, 'tp'), may hold values from -6 to 6
- lengths: int32 [768], P(('group', 'fsdp')), may hold values from 16 to 512, as said below
- weights: float32 [5120, 2048], P(('fsdp', 'tp')), may hold values from -0.078125 to 0.078125
- moment1: float32 [5120, 2048], P(('fsdp', 'tp')), may hold values from -3 to 3
- moment2: float32 [5120, 2048], P(('fsdp', 'tp')), may hold values from 0.25 to 4
- grad_parts: float32 [12, 5120, 2048], P('group', ('fsdp', 'tp')), may hold values from -2 to 2
Outputs:
- new_weights: float32 [5120, 2048], P(('fsdp', 'tp'))
- new_moment1: float32 [5120, 2048], P(('fsdp', 'tp'))
- new_moment2: float32 [5120, 2048], P(('fsdp', 'tp'))
- new_kv: bfloat16 [768, 4, 2048], P(('group', 'fsdp'), None, 'tp')
- context: bfloat16 [768, 4, 5120], P(('group', 'fsdp'), None, 'tp')
The draws below stay inside these ranges and needn't reach their ends.
Inputs may be any that keep to these rules, and one draw needn't show every extreme that they name: Row r's cache holds lengths[r] valid slots; some row holds 512.
All inputs are finite; a program needn't handle non-finite values.
Results may differ from the reference program's by a relative error of at most 0.0065.
Values may be sent and summed in bfloat16 or wider, within the bound.
A program may use at most 32 MiB of HBM per device.

```python
import math
import jax
import jax.numpy as jnp
from jax import lax

D = 5120
QH = 40
KVH = 8
HD = 128
STEPS = 4
R_DEV = 8
LMAX = 512
ROWS = 768
KVW = 2048
N_GROUP = 12


def draw_queries(key, part):
    sample = jax.random.truncated_normal(jax.random.fold_in(key, 11), -6.0, 6.0, (ROWS, STEPS, QH, HD), jnp.float32)
    return sample.reshape(ROWS, STEPS, QH * HD).astype(jnp.bfloat16)


def draw_cache_keys(key, part):
    sample = jax.random.truncated_normal(jax.random.fold_in(key, 13), -6.0, 6.0, (ROWS, LMAX, KVH, HD), jnp.float32)
    return sample.reshape(ROWS, LMAX, KVH * HD).astype(jnp.bfloat16)


def draw_lengths(key, part):
    blocks = ROWS // R_DEV
    device_caps = jax.random.randint(jax.random.fold_in(key, 21), (blocks,), LMAX // 4, LMAX + 1)
    cap_rows = jnp.repeat(device_caps, R_DEV)
    raw_draw = jax.random.randint(jax.random.fold_in(key, 22), (ROWS,), 0, 1 << 20)
    row_lengths = raw_draw % (cap_rows - 15) + 16
    return row_lengths.at[0].set(LMAX).astype(jnp.int32)


def level_of(stream_key, dims, cuts, low, largest):
    def one(axis_at, parts):
        draws = jax.random.uniform(jax.random.fold_in(jax.random.fold_in(stream_key, 6), axis_at), (parts,), jnp.float32, low / len(cuts), largest / len(cuts))
        return jnp.repeat(jnp.exp(draws), dims[axis_at] // parts).reshape((-1,) + (1,) * (len(dims) - axis_at - 1))

    loudness = one(*cuts[0])
    for cut in cuts[1:]:
        loudness = loudness * one(*cut)
    return loudness


def gaussian(own_key, dims, spread, bound, shards=(), kind=jnp.bfloat16):
    entries = jax.random.normal(own_key, dims, jnp.float32) * spread
    if len(shards) > 0:
        entries = level_of(own_key, dims, shards, -0.22, 0.18) * entries
    return jnp.clip(entries, min=-bound, max=bound).astype(kind)


def setup_inputs(seed: int = 0) -> dict:
    key_of = jax.random.split(jax.random.key(seed), 10)
    tokens = gaussian(key_of[0], (ROWS, STEPS, D), 1.0, 6.0, ((0, 96),))
    queries = draw_queries(jax.random.fold_in(key_of[9], 71), 0)
    cache_keys = draw_cache_keys(jax.random.fold_in(key_of[9], 71), 0)
    cache_values = gaussian(key_of[3], (ROWS, LMAX, KVH * HD), 1.0, 6.0, ((0, 96), (2, 8)))
    lengths = draw_lengths(jax.random.fold_in(key_of[9], 71), 0)
    weights = gaussian(key_of[5], (D, KVW), D ** -0.5, 0.078125, ((0, 64),), jnp.float32)
    moment1 = gaussian(key_of[6], (D, KVW), 0.5, 3.0, ((0, 64),), jnp.float32)
    moment2 = jnp.clip(jnp.exp(math.log(4.0) - 2.7725887 * jax.random.uniform(key_of[7], (D, KVW), jnp.float32) ** level_of(key_of[7], (D, KVW), ((0, 64),), -0.2, 0.2)), 0.25, 4.0)
    grad_parts = gaussian(key_of[8], (N_GROUP, D, KVW), 0.3, 2.0, ((0, 12), (1, 64)), jnp.float32)
    return {"tokens": tokens, "queries": queries, "cache_keys": cache_keys, "cache_values": cache_values, "lengths": lengths, "weights": weights, "moment1": moment1, "moment2": moment2, "grad_parts": grad_parts}


beta_one = 0.9
beta_two = 0.95
learning_rate = 0.004
decay_rate = 0.1
epsilon = 1e-08
correct_one = 1.0 - 0.9 ** 10
correct_two = 1.0 - 0.95 ** 10
masked_score = -1e+30

def adam_update(weights, moment1, moment2, gradient):
    new_moment1 = beta_one * moment1 + (1.0 - beta_one) * gradient
    new_moment2 = beta_two * moment2 + (1.0 - beta_two) * gradient * gradient
    direction = new_moment1 / correct_one / (jnp.sqrt(new_moment2 / correct_two) + epsilon)
    new_weights = weights - learning_rate * (direction + decay_rate * weights)
    return (new_weights, new_moment1, new_moment2)

def rotate_keys(keys, positions):
    half_width = keys.shape[-1] // 2
    frequency = jnp.power(jnp.float32(1000000.0), -2.0 * jnp.arange(half_width, dtype=jnp.float32) / keys.shape[-1])
    angles = positions[..., None] * frequency
    leading = keys[..., :half_width]
    trailing = keys[..., half_width:]
    cosine = jnp.cos(angles)
    sine_part = jnp.sin(angles)
    return jnp.concatenate([leading * cosine - trailing * sine_part, trailing * cosine + leading * sine_part], axis=-1)

def attend(block_args):
    query_rows, key_rows, value_rows, fresh_rows, row_lengths = block_args
    row_count = query_rows.shape[0]
    per_group = QH // KVH
    score_scale = 1.0 / math.sqrt(HD)
    grouped = query_rows.reshape(row_count, STEPS, KVH, per_group, HD).astype(jnp.float32)
    cached_keys = key_rows.reshape(row_count, LMAX, KVH, HD).astype(jnp.float32)
    cached_values = value_rows.reshape(row_count, LMAX, KVH, HD).astype(jnp.float32)
    fresh = fresh_rows.reshape(row_count, STEPS, KVH, 2, HD).astype(jnp.float32)
    cached_scores = jnp.einsum('risgd,rpsd->risgp', grouped, cached_keys) * score_scale
    in_range = jnp.arange(LMAX, dtype=jnp.int32)[None, :] < row_lengths[:, None]
    cached_scores = jnp.where(in_range[:, None, None, None, :], cached_scores, masked_score)
    new_scores = jnp.einsum('risgd,rjsd->risgj', grouped, fresh[:, :, :, 0]) * score_scale
    causal = jnp.arange(STEPS)[:, None] >= jnp.arange(STEPS)[None, :]
    new_scores = jnp.where(causal[None, :, None, None, :], new_scores, masked_score)
    all_scores = jnp.concatenate([cached_scores, new_scores], axis=-1)
    highest = lax.optimization_barrier(jnp.max(all_scores, axis=-1, keepdims=True))
    exponent = jnp.exp(all_scores - highest)
    probs = (exponent / lax.optimization_barrier(jnp.sum(exponent, axis=-1, keepdims=True))).astype(jnp.bfloat16)
    probs_wide = probs.astype(jnp.float32)
    context = jnp.einsum('risgp,rpsd->risgd', probs_wide[..., :LMAX], cached_values)
    context = context + jnp.einsum('risgj,rjsd->risgd', probs_wide[..., LMAX:], fresh[:, :, :, 1])
    return context.reshape(row_count, STEPS, QH * HD).astype(jnp.bfloat16)

def reference(tokens, queries, cache_keys, cache_values, lengths, weights, moment1, moment2, grad_parts):
    gradient = lax.optimization_barrier(jnp.sum(grad_parts, axis=0))
    new_weights, new_moment1, new_moment2 = adam_update(weights, moment1, moment2, gradient)
    rollout = new_weights.astype(jnp.bfloat16)
    projected = jnp.dot(tokens.reshape(ROWS * STEPS, D), rollout, preferred_element_type=jnp.float32)
    projected = projected.reshape(ROWS, STEPS, KVH, 2, HD)
    positions = (lengths[:, None] + jnp.arange(STEPS, dtype=jnp.int32)[None, :]).astype(jnp.float32)
    new_keys = rotate_keys(projected[:, :, :, 0], positions[:, :, None])
    new_kv = jnp.stack([new_keys, projected[:, :, :, 1]], axis=3).reshape(ROWS, STEPS, 2 * KVH * HD).astype(jnp.bfloat16)
    blocks = ROWS // R_DEV
    pieces = (queries.reshape(blocks, R_DEV, STEPS, QH * HD), cache_keys.reshape(blocks, R_DEV, LMAX, KVH * HD), cache_values.reshape(blocks, R_DEV, LMAX, KVH * HD), new_kv.reshape(blocks, R_DEV, STEPS, 2 * KVH * HD), lengths.reshape(blocks, R_DEV))
    context = lax.map(attend, pieces).reshape(ROWS, STEPS, QH * HD)
    return (new_weights, new_moment1, new_moment2, new_kv, context)
```

```python
import functools
import math

import jax
import jax.numpy as jnp
from jax import lax
from jax.experimental import pallas as pl
from jax.experimental.pallas import tpu as pltpu
from jax.sharding import PartitionSpec as P

QH = 40
KVH = 8
HD = 128
STEPS = 4
X_CHIPS = 4
CHUNK = 16

beta_one = 0.9
beta_two = 0.95
learning_rate = 0.004
decay_rate = 0.1
epsilon = 1e-08
correct_one = 1.0 - 0.9**10
correct_two = 1.0 - 0.95**10
masked_score = -1e30

MESH = pl.DeviceIdType.MESH


def adam_update(weights, moment1, moment2, gradient):
    new_moment1 = beta_one * moment1 + (1.0 - beta_one) * gradient
    new_moment2 = beta_two * moment2 + (1.0 - beta_two) * gradient * gradient
    direction = new_moment1 / correct_one / (jnp.sqrt(new_moment2 / correct_two) + epsilon)
    new_weights = weights - learning_rate * (direction + decay_rate * weights)
    return (new_weights, new_moment1, new_moment2)


def exchange_kernel(
    nx, nz, nf, nt,
    grad, weights, moment1, moment2, tokens,
    new_weights, new_moment1, new_moment2, projected,
    grad_v, w_v, m1_v, m2_v, gb, xr, zb, gf, wb, wf, tall, pf, pb, pr,
    grad_sem, in_sem, out_sem, xs, xq, zs, zq, gs, gq, ys, yq, ts, tq, ps, pq,
):
    group = lax.axis_index("group")
    f = lax.axis_index("fsdp")
    t = lax.axis_index("tp")
    x = lax.rem(group, nx)
    z = lax.div(group, nx)
    rows_all = grad_v.shape[0]
    cx = gb.shape[2]
    hc = wf.shape[2]
    depth = tall.shape[2]
    chunks = rows_all // CHUNK

    x_to = [z * nx + lax.rem(x + d, nx) for d in range(nx)]
    z_to = [lax.rem(z + d, nz) * nx + x for d in range(nz)]
    f_at = [lax.rem(f + d, nf) for d in range(nf)]
    t_at = [lax.rem(t + d, nt) for d in range(nt)]
    x_from = [lax.rem(x + nx - d, nx) for d in range(nx)]
    z_from = [lax.rem(z + nz - d, nz) for d in range(nz)]
    f_from = [lax.rem(f + nf - d, nf) for d in range(nf)]
    t_from = [lax.rem(t + nt - d, nt) for d in range(nt)]

    barrier = pltpu.get_barrier_semaphore()
    peers = (
        [(x_to[d], f, t) for d in range(1, nx)]
        + [(z_to[d], f, t) for d in range(1, nz)]
        + [(group, f, t_at[d]) for d in range(1, nt)]
        + [(group, f_at[d], t) for d in range(1, nf)]
    )
    for peer in peers:
        pl.semaphore_signal(barrier, inc=1, device_id=peer, device_id_type=MESH)

    def rows_of(r):
        return pl.ds(r * CHUNK, CHUNK)

    loads = [
        pltpu.make_async_copy(grad.at[0, rows_of(r)], grad_v.at[rows_of(r)], grad_sem.at[r])
        for r in range(chunks)
    ]
    for load in loads:
        load.start()
    own_tokens = pltpu.make_async_copy(
        tokens.at[:, pl.ds(pl.multiple_of(f * depth, 128), depth)], tall.at[f], in_sem.at[3]
    )
    own_tokens.start()
    state = [
        pltpu.make_async_copy(src, dst, in_sem.at[i])
        for i, (src, dst) in enumerate(((weights, w_v), (moment1, m1_v), (moment2, m2_v)))
    ]
    for load in state:
        load.start()

    def cast(r):
        loads[r].wait()
        for i in range(nx):
            gb[i, rows_of(r)] = grad_v[rows_of(r), pl.ds(i * cx, cx)].astype(jnp.bfloat16)

    def remote(src, dst, send, recv, device):
        return pltpu.make_async_remote_copy(
            src_ref=src, dst_ref=dst, send_sem=send, recv_sem=recv,
            device_id=device, device_id_type=MESH,
        )

    started = []

    def send(*args):
        copy = remote(*args)
        copy.start()
        started.append(copy)

    def arrive(dst, send_sem, recv_sem):
        remote(dst, dst, send_sem, recv_sem, (group, f, t)).wait_recv()

    def scatter_x(r):
        for d in range(1, nx):
            send(
                gb.at[lax.rem(x + d, nx), rows_of(r)], xr.at[d - 1, rows_of(r)],
                xs.at[r, d - 1], xq.at[r, d - 1], (x_to[d], f, t),
            )

    def exchange_z(r):
        total = gb[x, rows_of(r)].astype(jnp.float32)
        for d in range(1, nx):
            arrive(xr.at[d - 1, rows_of(r)], xs.at[r, d - 1], xq.at[r, d - 1])
            total += xr[d - 1, rows_of(r)].astype(jnp.float32)
        zb[z, rows_of(r)] = total.astype(jnp.bfloat16)
        for d in range(1, nz):
            send(
                zb.at[z, rows_of(r)], zb.at[z, rows_of(r)],
                zs.at[r, d - 1], zq.at[r, d - 1], (z_to[d], f, t),
            )

    def gather_x(r):
        for d in range(1, nz):
            arrive(zb.at[z_from[d], rows_of(r)], zs.at[r, d - 1], zq.at[r, d - 1])
        total = zb[0, rows_of(r)].astype(jnp.float32)
        for i in range(1, nz):
            total += zb[i, rows_of(r)].astype(jnp.float32)
        gf[x, rows_of(r)] = total.astype(jnp.bfloat16)
        for d in range(1, nx):
            send(
                gf.at[x, rows_of(r)], gf.at[x, rows_of(r)],
                gs.at[r, d - 1], gq.at[r, d - 1], (x_to[d], f, t),
            )

    t_order = sorted(range(1, nt), key=lambda d: -min(d, nt - d))

    def update(r):
        for d in range(1, nx):
            arrive(gf.at[x_from[d], rows_of(r)], gs.at[r, d - 1], gq.at[r, d - 1])
        for i in range(nx):
            columns = pl.ds(i * cx, cx)
            new_w, new_1, new_2 = adam_update(
                w_v[rows_of(r), columns],
                m1_v[rows_of(r), columns],
                m2_v[rows_of(r), columns],
                gf[i, rows_of(r)].astype(jnp.float32),
            )
            w_v[rows_of(r), columns] = new_w
            m1_v[rows_of(r), columns] = new_1
            m2_v[rows_of(r), columns] = new_2
            rounded = new_w.astype(jnp.bfloat16)
            for j in range(cx // hc):
                wb[i * (cx // hc) + j, rows_of(r)] = rounded[:, j * hc : (j + 1) * hc]
        for d in t_order:
            send(
                wb.at[t_at[d], rows_of(r)], wf.at[t, rows_of(r)],
                ys.at[r, d - 1], yq.at[r, d - 1], (group, f, t_at[d]),
            )
        wf[t, rows_of(r)] = wb[t, rows_of(r)]

    for r in range(chunks):
        cast(r)
    pl.semaphore_wait(barrier, len(peers))
    for r in range(chunks):
        scatter_x(r)
    for r in range(chunks):
        exchange_z(r)
    for d in range(1, nf):
        send(
            tokens.at[:, pl.ds(pl.multiple_of(f_at[d] * depth, 128), depth)], tall.at[f],
            ts.at[d - 1], tq.at[d - 1], (group, f_at[d], t),
        )
    for load in state:
        load.wait()
    gather_x(0)
    for r in range(1, chunks):
        gather_x(r)
        update(r - 1)
    update(chunks - 1)

    stores = [
        pltpu.make_async_copy(src, dst, out_sem.at[i])
        for i, (src, dst) in enumerate(
            ((w_v, new_weights), (m1_v, new_moment1), (m2_v, new_moment2))
        )
    ]
    for store in stores:
        store.start()

    own_tokens.wait()
    for d in range(1, nf):
        arrive(tall.at[f_from[d]], ts.at[d - 1], tq.at[d - 1])
    for r in range(chunks):
        for d in range(1, nt):
            arrive(wf.at[t_from[d], rows_of(r)], ys.at[r, d - 1], yq.at[r, d - 1])
    partial = jnp.dot(
        tall[...].reshape(-1, depth), wf[...].reshape(depth, hc), preferred_element_type=jnp.float32
    ).reshape(pf.shape)
    pb[...] = partial.astype(jnp.bfloat16)
    for d in range(1, nf):
        send(
            pb.at[f_at[d]], pr.at[f], ps.at[d - 1], pq.at[d - 1], (group, f_at[d], t)
        )
    pf[...] = partial
    total = pf[f]
    for d in range(1, nf):
        arrive(pr.at[f_from[d]], ps.at[d - 1], pq.at[d - 1])
        total += pr[f_from[d]].astype(jnp.float32)
    projected[...] = total
    for copy in started:
        copy.wait_send()
    for store in stores:
        store.wait()


def exchange(sizes, grad_parts, weights, moment1, moment2, tokens):
    nx, nz, nf, nt = sizes
    rows, columns = weights.shape
    token_rows = tokens.shape[0]
    cx = columns // nx
    hc = columns // nt
    depth = nt * rows
    chunks = rows // CHUNK
    dma = pltpu.SemaphoreType.DMA
    f32 = jnp.float32
    bf16 = jnp.bfloat16
    any_space = pl.BlockSpec(memory_space=pl.ANY)
    return pl.pallas_call(
        functools.partial(exchange_kernel, nx, nz, nf, nt),
        out_shape=[jax.ShapeDtypeStruct((rows, columns), f32)] * 3
        + [jax.ShapeDtypeStruct((token_rows, hc), f32)],
        in_specs=[any_space] * 5,
        out_specs=[any_space] * 3 + [pl.BlockSpec(memory_space=pltpu.VMEM)],
        scratch_shapes=[pltpu.VMEM((rows, columns), f32)] * 4
        + [
            pltpu.VMEM((nx, rows, cx), bf16),
            pltpu.VMEM((nx - 1, rows, cx), bf16),
            pltpu.VMEM((nz, rows, cx), bf16),
            pltpu.VMEM((nx, rows, cx), bf16),
            pltpu.VMEM((nt, rows, hc), bf16),
            pltpu.VMEM((nt, rows, hc), bf16),
            pltpu.VMEM((nf, token_rows, depth), bf16),
            pltpu.VMEM((nf, token_rows, hc), f32),
            pltpu.VMEM((nf, token_rows, hc), bf16),
            pltpu.VMEM((nf, token_rows, hc), bf16),
            dma((chunks,)),
            dma((4,)),
            dma((3,)),
        ]
        + [dma((chunks, nx - 1))] * 2
        + [dma((chunks, nz - 1))] * 2
        + [dma((chunks, nx - 1))] * 2
        + [dma((chunks, nt - 1))] * 2
        + [dma((nf - 1,))] * 4,
        compiler_params=pltpu.CompilerParams(
            collective_id=0, has_side_effects=True, vmem_limit_bytes=32 << 20
        ),
    )(grad_parts, weights, moment1, moment2, tokens)


def rotate_keys(keys, positions):
    half_width = keys.shape[-1] // 2
    frequency = jnp.power(
        jnp.float32(1000000.0), -2.0 * jnp.arange(half_width, dtype=jnp.float32) / keys.shape[-1]
    )
    angles = positions[..., None] * frequency
    leading = keys[..., :half_width]
    trailing = keys[..., half_width:]
    cosine = jnp.cos(angles)
    sine_part = jnp.sin(angles)
    return jnp.concatenate(
        [leading * cosine - trailing * sine_part, trailing * cosine + leading * sine_part], axis=-1
    )


def shards(
    sizes, tokens, queries, cache_keys, cache_values, lengths, weights, moment1, moment2, grad_parts
):
    row_count = tokens.shape[0]
    token_rows = tokens.reshape(row_count * STEPS, tokens.shape[2])
    new_weights, new_moment1, new_moment2, projected = exchange(
        sizes, grad_parts, weights, moment1, moment2, token_rows
    )
    head_cols = projected.shape[1]
    kv_heads = head_cols // (2 * HD)
    projected = projected.reshape(row_count, STEPS, kv_heads, 2, HD)
    positions = (lengths[:, None] + jnp.arange(STEPS, dtype=jnp.int32)[None, :]).astype(jnp.float32)
    new_keys = rotate_keys(projected[:, :, :, 0], positions[:, :, None])
    fresh = jnp.stack([new_keys, projected[:, :, :, 1]], axis=3).astype(jnp.bfloat16)
    new_kv = fresh.reshape(row_count, STEPS, head_cols)
    per_group = QH // KVH
    score_scale = 1.0 / math.sqrt(HD)
    span_length = cache_keys.shape[1]
    grouped = queries.reshape(row_count, STEPS, kv_heads, per_group, HD)
    cached_keys = cache_keys.reshape(row_count, span_length, kv_heads, HD)
    cached_values = cache_values.reshape(row_count, span_length, kv_heads, HD)
    new_scores = (
        jnp.einsum(
            "risgd,rjsd->risgj", grouped, fresh[:, :, :, 0], preferred_element_type=jnp.float32
        )
        * score_scale
    )
    causal = jnp.arange(STEPS)[:, None] >= jnp.arange(STEPS)[None, :]
    new_scores = jnp.where(causal[None, :, None, None, :], new_scores, masked_score)
    scores = (
        jnp.einsum("risgd,rpsd->risgp", grouped, cached_keys, preferred_element_type=jnp.float32)
        * score_scale
    )
    in_range = jnp.arange(span_length, dtype=jnp.int32)[None, :] < lengths[:, None]
    all_scores = jnp.concatenate(
        [jnp.where(in_range[:, None, None, None, :], scores, masked_score), new_scores], axis=-1
    )
    highest = jnp.max(all_scores, axis=-1, keepdims=True)
    exponent = jnp.exp(all_scores - highest)
    probs = (exponent / jnp.sum(exponent, axis=-1, keepdims=True)).astype(jnp.bfloat16)
    context = jnp.einsum(
        "risgp,rpsd->risgd",
        probs[..., :span_length],
        cached_values,
        preferred_element_type=jnp.float32,
    )
    context = context + jnp.einsum(
        "risgj,rjsd->risgd",
        probs[..., span_length:],
        fresh[:, :, :, 1],
        preferred_element_type=jnp.float32,
    )
    context = context.reshape(row_count, STEPS, kv_heads * per_group * HD).astype(jnp.bfloat16)
    return (new_weights, new_moment1, new_moment2, new_kv, context)


def solution(mesh):
    in_specs = (
        P(("group", "fsdp"), None, None),
        P(("group", "fsdp"), None, "tp"),
        P(("group", "fsdp"), None, "tp"),
        P(("group", "fsdp"), None, "tp"),
        P(("group", "fsdp")),
        P(("fsdp", "tp"), None),
        P(("fsdp", "tp"), None),
        P(("fsdp", "tp"), None),
        P("group", ("fsdp", "tp"), None),
    )
    out_specs = (
        P(("fsdp", "tp"), None),
        P(("fsdp", "tp"), None),
        P(("fsdp", "tp"), None),
        P(("group", "fsdp"), None, "tp"),
        P(("group", "fsdp"), None, "tp"),
    )
    nx = X_CHIPS
    sizes = (nx, mesh.shape["group"] // nx, mesh.shape["fsdp"], mesh.shape["tp"])
    return jax.shard_map(
        functools.partial(shards, sizes),
        mesh=mesh,
        in_specs=in_specs,
        out_specs=out_specs,
        check_vma=False,
    )
```

```python
import functools
import math

import jax
import jax.numpy as jnp
from jax import lax
from jax.experimental import pallas as pl
from jax.experimental.pallas import tpu as pltpu
from jax.sharding import PartitionSpec as P

QH = 40
KVH = 8
HD = 128
STEPS = 4
X_CHIPS = 4
CHUNK = 16

beta_one = 0.9
beta_two = 0.95
learning_rate = 0.004
decay_rate = 0.1
epsilon = 1e-08
correct_one = 1.0 - 0.9**10
correct_two = 1.0 - 0.95**10
masked_score = -1e30
SCORE_SCALE = 1.0 / math.sqrt(HD)

MESH = pl.DeviceIdType.MESH


def adam_update(weights, moment1, moment2, gradient):
    new_moment1 = beta_one * moment1 + (1.0 - beta_one) * gradient
    new_moment2 = beta_two * moment2 + (1.0 - beta_two) * gradient * gradient
    direction = new_moment1 / correct_one / (jnp.sqrt(new_moment2 / correct_two) + epsilon)
    new_weights = weights - learning_rate * (direction + decay_rate * weights)
    return (new_weights, new_moment1, new_moment2)


def exchange_kernel(
    nx, nz, nf, nt,
    grad, weights, moment1, moment2, tokens, queries, cache_keys, cache_values, lengths,
    new_w, new_1, new_2, projected, query_rows, top, mass, cached, cosine, sine,
    grad_v, w_v, m1_v, m2_v, tok_v, q_v, k_v, v_v, len_s, row_v, tb, qf,
    gb, xr, zb, gf, wb, wf, tall, pf, pb, pr,
    grad_sem, in_sem, xs, xq, zs, zq, gs, gq, ys, yq, ts, tq, ps, pq,
):
    group = lax.axis_index("group")
    f = lax.axis_index("fsdp")
    t = lax.axis_index("tp")
    x = lax.rem(group, nx)
    z = lax.div(group, nx)
    rows_all = grad_v.shape[0]
    cx = gb.shape[2]
    hc = wf.shape[2]
    depth = tall.shape[2]
    chunks = rows_all // CHUNK
    f32 = jnp.float32
    bf16 = jnp.bfloat16

    x_to = [z * nx + lax.rem(x + d, nx) for d in range(nx)]
    z_to = [lax.rem(z + d, nz) * nx + x for d in range(nz)]
    f_at = [lax.rem(f + d, nf) for d in range(nf)]
    t_at = [lax.rem(t + d, nt) for d in range(nt)]
    x_from = [lax.rem(x + nx - d, nx) for d in range(nx)]
    z_from = [lax.rem(z + nz - d, nz) for d in range(nz)]
    f_from = [lax.rem(f + nf - d, nf) for d in range(nf)]
    t_from = [lax.rem(t + nt - d, nt) for d in range(nt)]

    barrier = pltpu.get_barrier_semaphore()
    peers = (
        [(z_to[d], f, t) for d in range(1, nz)]
        + [(group, f, t_at[d]) for d in range(1, nt)]
        + [(group, f_at[d], t) for d in range(1, nf)]
        + [(x_to[d], f, t) for d in range(1, nx)]
    )
    for peer in peers:
        pl.semaphore_signal(barrier, inc=1, device_id=peer, device_id_type=MESH)

    def rows_of(r):
        return pl.ds(r * CHUNK, CHUNK)

    loads = [
        pltpu.make_async_copy(grad.at[0, rows_of(r)], grad_v.at[rows_of(r)], grad_sem.at[r])
        for r in range(chunks)
    ]
    others = [
        pltpu.make_async_copy(src, dst, in_sem.at[i])
        for i, (src, dst) in enumerate(
            (
                (tokens, tok_v), (queries, q_v), (lengths, len_s), (cache_keys, k_v),
                (cache_values, v_v), (weights, w_v), (moment1, m1_v), (moment2, m2_v),
            )
        )
    ]
    for load in loads + others:
        load.start()

    def cast(r):
        loads[r].wait()
        for i in range(nx):
            gb[i, rows_of(r)] = grad_v[rows_of(r), pl.ds(i * cx, cx)].astype(bf16)

    def remote(src, dst, send, recv, device):
        return pltpu.make_async_remote_copy(
            src_ref=src, dst_ref=dst, send_sem=send, recv_sem=recv,
            device_id=device, device_id_type=MESH,
        )

    started = []

    def send(*args):
        copy = remote(*args)
        copy.start()
        started.append(copy)

    def arrive(dst, send_sem, recv_sem):
        remote(dst, dst, send_sem, recv_sem, (group, f, t)).wait_recv()

    def scatter_x(r):
        for d in range(1, nx):
            send(
                gb.at[lax.rem(x + d, nx), rows_of(r)], xr.at[d - 1, rows_of(r)],
                xs.at[r, d - 1], xq.at[r, d - 1], (x_to[d], f, t),
            )

    def exchange_z(r):
        total = gb[x, rows_of(r)].astype(f32)
        for d in range(1, nx):
            arrive(xr.at[d - 1, rows_of(r)], xs.at[r, d - 1], xq.at[r, d - 1])
            total += xr[d - 1, rows_of(r)].astype(f32)
        zb[z, rows_of(r)] = total.astype(bf16)
        for d in range(1, nz):
            send(
                zb.at[z, rows_of(r)], zb.at[z, rows_of(r)],
                zs.at[r, d - 1], zq.at[r, d - 1], (z_to[d], f, t),
            )

    def gather_x(r):
        for d in range(1, nz):
            arrive(zb.at[z_from[d], rows_of(r)], zs.at[r, d - 1], zq.at[r, d - 1])
        total = zb[0, rows_of(r)].astype(f32)
        for i in range(1, nz):
            total += zb[i, rows_of(r)].astype(f32)
        gf[x, rows_of(r)] = total.astype(bf16)
        for d in range(1, nx):
            send(
                gf.at[x, rows_of(r)], gf.at[x, rows_of(r)],
                gs.at[r, d - 1], gq.at[r, d - 1], (x_to[d], f, t),
            )

    t_order = sorted(range(1, nt), key=lambda d: -min(d, nt - d))

    def update(r):
        for d in range(1, nx):
            arrive(gf.at[x_from[d], rows_of(r)], gs.at[r, d - 1], gq.at[r, d - 1])
        for i in range(nx):
            columns = pl.ds(i * cx, cx)
            w, one, two = adam_update(
                w_v[rows_of(r), columns],
                m1_v[rows_of(r), columns],
                m2_v[rows_of(r), columns],
                gf[i, rows_of(r)].astype(f32),
            )
            new_w[rows_of(r), columns] = w
            new_1[rows_of(r), columns] = one
            new_2[rows_of(r), columns] = two
            rounded = w.astype(bf16)
            for j in range(cx // hc):
                wb[i * (cx // hc) + j, rows_of(r)] = rounded[:, j * hc : (j + 1) * hc]
        for d in t_order:
            send(
                wb.at[t_at[d], rows_of(r)], wf.at[t, rows_of(r)],
                ys.at[r, d - 1], yq.at[r, d - 1], (group, f, t_at[d]),
            )
        wf[t, rows_of(r)] = wb[t, rows_of(r)]

    def lay_out_tokens():
        others[0].wait()
        for i in range(nf):
            for row in range(tok_v.shape[0]):
                row_v[pl.ds(row * STEPS, STEPS)] = tok_v[row, :, pl.ds(i * depth, depth)].astype(f32)
            tb[i] = row_v[...].astype(bf16)
        tall[f] = tb[f]

    def attend_cache():
        for load in others[1:5]:
            load.wait()
        heads = QH // KVH
        qf[:, pl.ds(heads * STEPS, 4)] = jnp.zeros((qf.shape[0], 4, HD), f32)
        for head in range(heads):
            qf[:, pl.ds(head * STEPS, STEPS)] = q_v[:, :, pl.ds(head * HD, HD)].astype(f32)
        pad = qf.shape[1]
        query_rows[...] = qf[...].reshape(-1, HD).astype(bf16)
        slots = lax.broadcasted_iota(jnp.int32, (pad, k_v.shape[1]), 1)
        for row in range(qf.shape[0]):
            scores = lax.dot_general(
                qf[row].astype(bf16), k_v[row], (((1,), (1,)), ((), ())),
                preferred_element_type=f32,
            ) * SCORE_SCALE
            scores = jnp.where(slots < len_s[row], scores, masked_score)
            highest = jnp.max(scores, axis=-1, keepdims=True)
            exponent = jnp.exp(scores - highest)
            out = pl.ds(row * pad, pad)
            top[out] = jnp.broadcast_to(highest, (pad, HD))
            mass[out] = jnp.broadcast_to(jnp.sum(exponent, axis=-1, keepdims=True), (pad, HD))
            cached[out] = jnp.dot(exponent.astype(bf16), v_v[row], preferred_element_type=f32)
        token_rows = qf.shape[0] * STEPS
        at = lax.broadcasted_iota(jnp.int32, (token_rows, HD), 0)
        lane = lax.broadcasted_iota(jnp.int32, (token_rows, HD), 1)
        position = lax.rem(at, STEPS)
        for row in range(qf.shape[0]):
            position += jnp.where(lax.div(at, STEPS) == row, len_s[row], 0)
        power = lax.rem(lane, HD // 2).astype(f32) * (-2.0 / HD)
        angle = position.astype(f32) * jnp.exp(power * math.log(1000000.0))
        cosine[...] = jnp.cos(angle)
        turn = jnp.sin(angle)
        sine[...] = jnp.where(lane < HD // 2, -turn, turn)

    for r in range(chunks):
        cast(r)
    pl.semaphore_wait(barrier, len(peers))
    for r in range(chunks):
        scatter_x(r)
    lay_out_tokens()
    attend_cache()
    for r in range(chunks):
        exchange_z(r)
    for d in range(1, nf):
        send(tb.at[f_at[d]], tall.at[f], ts.at[d - 1], tq.at[d - 1], (group, f_at[d], t))
    for load in others[5:]:
        load.wait()
    gather_x(0)
    for r in range(1, chunks):
        gather_x(r)
        update(r - 1)
    update(chunks - 1)

    for d in range(1, nf):
        arrive(tall.at[f_from[d]], ts.at[d - 1], tq.at[d - 1])
    for r in range(chunks):
        for d in range(1, nt):
            arrive(wf.at[t_from[d], rows_of(r)], ys.at[r, d - 1], yq.at[r, d - 1])
    partial = jnp.dot(
        tall[...].reshape(-1, depth), wf[...].reshape(depth, hc), preferred_element_type=f32
    ).reshape(pf.shape)
    pb[...] = partial.astype(bf16)
    for d in range(1, nf):
        send(pb.at[f_at[d]], pr.at[f], ps.at[d - 1], pq.at[d - 1], (group, f_at[d], t))
    pf[...] = partial
    total = pf[f]
    for d in range(1, nf):
        arrive(pr.at[f_from[d]], ps.at[d - 1], pq.at[d - 1])
        total += pr[f_from[d]].astype(f32)
    projected[...] = total
    for copy in started:
        copy.wait_send()


def finish_kernel(
    new_w, new_1, new_2, projected, query_rows, top, mass, cached, cosine, sine,
    w_out, m1_out, m2_out, kv_out, context_out, kv_v, context_v, merged, sem,
):
    f32 = jnp.float32
    bf16 = jnp.bfloat16
    stores = [
        pltpu.make_async_copy(src, dst, sem.at[i])
        for i, (src, dst) in enumerate(
            ((new_w, w_out), (new_1, m1_out), (new_2, m2_out), (kv_v, kv_out), (context_v, context_out))
        )
    ]
    for store in stores[:3]:
        store.start()
    rows = kv_v.shape[0]
    token_rows = projected.shape[0]
    pad = query_rows.shape[0] // rows
    keys = projected[:, :HD]
    keys = keys * cosine[...] + pltpu.roll(keys, HD // 2, 1) * sine[...]
    values = projected[:, HD:]
    for row in range(rows):
        span = slice(row * STEPS, (row + 1) * STEPS)
        kv_v[row, :, :HD] = keys[span].astype(bf16)
        kv_v[row, :, HD:] = values[span].astype(bf16)
    stores[3].start()
    scores = lax.dot_general(
        query_rows[...], keys.astype(bf16), (((1,), (1,)), ((), ())), preferred_element_type=f32
    ) * SCORE_SCALE
    at = lax.broadcasted_iota(jnp.int32, scores.shape, 0)
    new = lax.broadcasted_iota(jnp.int32, scores.shape, 1)
    seen = (lax.div(at, pad) == lax.div(new, STEPS)) & (lax.rem(new, STEPS) <= lax.rem(at, STEPS))
    scores = jnp.where(seen, scores, masked_score)
    highest = jnp.maximum(jnp.max(scores, axis=-1, keepdims=True), top[...])
    exponent = jnp.exp(scores - highest[:, :token_rows])
    kept = jnp.exp(top[...] - highest)
    weight = kept * mass[...] + jnp.sum(exponent, axis=-1, keepdims=True)
    context = kept * cached[...] + jnp.dot(
        exponent.astype(bf16), values.astype(bf16), preferred_element_type=f32
    )
    merged[...] = (context / weight).reshape(merged.shape)
    for head in range(QH // KVH):
        context_v[:, :, pl.ds(head * HD, HD)] = merged[:, pl.ds(head * STEPS, STEPS)].astype(bf16)
    stores[4].start()
    for store in stores:
        store.wait()


def shards(
    sizes, tokens, queries, cache_keys, cache_values, lengths, weights, moment1, moment2, grad_parts
):
    nx, nz, nf, nt = sizes
    rows, columns = weights.shape
    row_count = tokens.shape[0]
    token_rows = row_count * STEPS
    span = cache_keys.shape[1]
    cx = columns // nx
    hc = columns // nt
    depth = nt * rows
    chunks = rows // CHUNK
    pad = 8 * pl.cdiv(STEPS * (QH // KVH), 8)
    dma = pltpu.SemaphoreType.DMA
    f32 = jnp.float32
    bf16 = jnp.bfloat16
    hbm = pl.BlockSpec(memory_space=pltpu.HBM)
    vmem = pl.BlockSpec(memory_space=pltpu.VMEM)
    shape = jax.ShapeDtypeStruct
    block = shape((rows, columns), f32)
    held = pl.pallas_call(
        functools.partial(exchange_kernel, nx, nz, nf, nt),
        out_shape=[block] * 3
        + [shape((token_rows, hc), f32), shape((row_count * pad, HD), bf16)]
        + [shape((row_count * pad, HD), f32)] * 3
        + [shape((token_rows, HD), f32)] * 2,
        in_specs=[hbm] * 9,
        out_specs=[vmem] * 10,
        scratch_shapes=[pltpu.VMEM((rows, columns), f32)] * 4
        + [
            pltpu.VMEM(tokens.shape, bf16),
            pltpu.VMEM(queries.shape, bf16),
            pltpu.VMEM(cache_keys.shape, bf16),
            pltpu.VMEM(cache_values.shape, bf16),
            pltpu.SMEM(lengths.shape, jnp.int32),
            pltpu.VMEM((token_rows, depth), f32),
            pltpu.VMEM((nf, token_rows, depth), bf16),
            pltpu.VMEM((row_count, pad, HD), f32),
            pltpu.VMEM((nx, rows, cx), bf16),
            pltpu.VMEM((nx - 1, rows, cx), bf16),
            pltpu.VMEM((nz, rows, cx), bf16),
            pltpu.VMEM((nx, rows, cx), bf16),
            pltpu.VMEM((nt, rows, hc), bf16),
            pltpu.VMEM((nt, rows, hc), bf16),
            pltpu.VMEM((nf, token_rows, depth), bf16),
            pltpu.VMEM((nf, token_rows, hc), f32),
            pltpu.VMEM((nf, token_rows, hc), bf16),
            pltpu.VMEM((nf, token_rows, hc), bf16),
            dma((chunks,)),
            dma((8,)),
        ]
        + [dma((chunks, nx - 1))] * 2
        + [dma((chunks, nz - 1))] * 2
        + [dma((chunks, nx - 1))] * 2
        + [dma((chunks, nt - 1))] * 2
        + [dma((nf - 1,))] * 4,
        compiler_params=pltpu.CompilerParams(
            collective_id=0, has_side_effects=True, vmem_limit_bytes=40 << 20
        ),
        name="exchange",
    )(
        *(
            pltpu.with_memory_space_constraint(operand, pltpu.HBM)
            for operand in (
                grad_parts, weights, moment1, moment2, tokens, queries, cache_keys, cache_values, lengths
            )
        )
    )
    return pl.pallas_call(
        finish_kernel,
        out_shape=[block] * 3
        + [shape((row_count, STEPS, hc), bf16), shape(queries.shape, bf16)],
        in_specs=[vmem] * 10,
        out_specs=[hbm] * 5,
        scratch_shapes=[
            pltpu.VMEM((row_count, STEPS, hc), bf16),
            pltpu.VMEM(queries.shape, bf16),
            pltpu.VMEM((row_count, pad, HD), f32),
            dma((5,)),
        ],
        compiler_params=pltpu.CompilerParams(vmem_limit_bytes=16 << 20),
        name="finish",
    )(*held)


def solution(mesh):
    in_specs = (
        P(("group", "fsdp"), None, None),
        P(("group", "fsdp"), None, "tp"),
        P(("group", "fsdp"), None, "tp"),
        P(("group", "fsdp"), None, "tp"),
        P(("group", "fsdp")),
        P(("fsdp", "tp"), None),
        P(("fsdp", "tp"), None),
        P(("fsdp", "tp"), None),
        P("group", ("fsdp", "tp"), None),
    )
    out_specs = (
        P(("fsdp", "tp"), None),
        P(("fsdp", "tp"), None),
        P(("fsdp", "tp"), None),
        P(("group", "fsdp"), None, "tp"),
        P(("group", "fsdp"), None, "tp"),
    )
    nx = X_CHIPS
    sizes = (nx, mesh.shape["group"] // nx, mesh.shape["fsdp"], mesh.shape["tp"])
    return jax.shard_map(
        functools.partial(shards, sizes),
        mesh=mesh,
        in_specs=in_specs,
        out_specs=out_specs,
        check_vma=False,
    )
```

```python
import functools
import math

import jax
import jax.numpy as jnp
from jax import lax
from jax.experimental import pallas as pl
from jax.experimental.pallas import tpu as pltpu
from jax.sharding import PartitionSpec as P

QH = 40
KVH = 8
HD = 128
STEPS = 4
X_CHIPS = 4
SPAN = 1
CHUNK = 16

beta_one = 0.9
beta_two = 0.95
learning_rate = 0.004
decay_rate = 0.1
epsilon = 1e-08
correct_one = 1.0 - 0.9**10
correct_two = 1.0 - 0.95**10
masked_score = -1e30
SCORE_SCALE = 1.0 / math.sqrt(HD)

MESH = pl.DeviceIdType.MESH


def adam_update(weights, moment1, moment2, gradient):
    new_moment1 = beta_one * moment1 + (1.0 - beta_one) * gradient
    new_moment2 = beta_two * moment2 + (1.0 - beta_two) * gradient * gradient
    direction = new_moment1 / correct_one / (jnp.sqrt(new_moment2 / correct_two) + epsilon)
    new_weights = weights - learning_rate * (direction + decay_rate * weights)
    return (new_weights, new_moment1, new_moment2)


def flip(value, bits):
    out = value
    for b in range(bits.bit_length()):
        if (bits >> b) % 2:
            out = out + (1 << b) * (1 - 2 * lax.rem(lax.div(value, 1 << b), 2))
    return out


def exchange_kernel(
    nx, nz, nf, nt,
    grad, weights, moment1, moment2, tokens, queries, cache_keys, cache_values, lengths,
    new_w, new_1, new_2, projected, query_rows, top, mass, cached, cosine, sine,
    grad_v, w_v, m1_v, m2_v, tok_v, q_v, k_v, v_v, len_s, row_v, tb, qf,
    gb, xr, zb, gf, wb, wf, tall, pf, pb, pr,
    grad_sem, in_sem, xs, xq, zs, zq, gs, gq, ys, yq, ts, tq, ps, pq,
):
    group = lax.axis_index("group")
    f = lax.axis_index("fsdp")
    t = lax.axis_index("tp")
    x = lax.rem(group, nx)
    z = lax.div(group, nx)
    rows_all = grad_v.shape[0]
    hc = wf.shape[2]
    hx = nt // nx
    depth = tall.shape[2]
    chunks = rows_all // CHUNK
    f32 = jnp.float32
    bf16 = jnp.bfloat16

    x_to = [z * nx + lax.rem(x + d, nx) for d in range(nx)]
    z_to = [lax.rem(z + d, nz) * nx + x for d in range(nz)]
    f_by = [flip(f, k) for k in range(nf)]
    t_at = [lax.rem(t + d, nt) for d in range(nt)]
    x_from = [lax.rem(x + nx - d, nx) for d in range(nx)]
    z_from = [lax.rem(z + nz - d, nz) for d in range(nz)]

    barrier = pltpu.get_barrier_semaphore()
    peers = (
        [(z_to[d], f, t) for d in range(1, nz)]
        + [(group, f, t_at[d]) for d in range(1, nt)]
        + [(group, f_by[k], t) for k in range(1, nf)]
        + [(x_to[d], f, t) for d in range(1, nx)]
    )
    for peer in peers:
        pl.semaphore_signal(barrier, inc=1, device_id=peer, device_id_type=MESH)

    def rows_of(r):
        return pl.ds(r * CHUNK, CHUNK)

    loads = [
        pltpu.make_async_copy(grad.at[0, rows_of(r)], grad_v.at[rows_of(r)], grad_sem.at[r])
        for r in range(chunks)
    ]
    others = [
        pltpu.make_async_copy(src, dst, in_sem.at[i])
        for i, (src, dst) in enumerate(
            (
                (tokens, tok_v), (queries, q_v), (lengths, len_s), (cache_keys, k_v),
                (cache_values, v_v), (weights, w_v), (moment1, m1_v), (moment2, m2_v),
            )
        )
    ]
    for load in loads:
        load.start()

    def cast(r):
        loads[r].wait()
        for h in range(nx * hx):
            gb[h % nx, h // nx, rows_of(r)] = grad_v[rows_of(r), pl.ds(h * hc, hc)].astype(bf16)

    def remote(src, dst, send, recv, device):
        return pltpu.make_async_remote_copy(
            src_ref=src, dst_ref=dst, send_sem=send, recv_sem=recv,
            device_id=device, device_id_type=MESH,
        )

    started = []

    def send(*args):
        copy = remote(*args)
        copy.start()
        started.append(copy)

    def arrive(dst, send_sem, recv_sem):
        remote(dst, dst, send_sem, recv_sem, (group, f, t)).wait_recv()

    def part(at_x, r):
        return lax.rem(at_x - r - t + nx * (chunks + nt), nx)

    def scatter_x(u, r, es):
        for d in range(1, nx):
            send(
                gb.at[part(lax.rem(x + d, nx), r), es, rows_of(r)], xr.at[d - 1, es, rows_of(r)],
                xs.at[u, d - 1], xq.at[u, d - 1], (x_to[d], f, t),
            )

    def exchange_z(u, r, es):
        total = gb[part(x, r), es, rows_of(r)].astype(f32)
        for d in range(1, nx):
            arrive(xr.at[d - 1, es, rows_of(r)], xs.at[u, d - 1], xq.at[u, d - 1])
            total += xr[d - 1, es, rows_of(r)].astype(f32)
        zb[z, es, rows_of(r)] = total.astype(bf16)
        piece = zb.at[z, es, rows_of(r)]
        for d in range(1, nz):
            send(piece, piece, zs.at[u, d - 1], zq.at[u, d - 1], (z_to[d], f, t))

    def update(r, h, gradient):
        columns = pl.ds(pl.multiple_of(h * hc, hc), hc)
        w, one, two = adam_update(
            w_v[rows_of(r), columns], m1_v[rows_of(r), columns], m2_v[rows_of(r), columns], gradient
        )
        new_w[rows_of(r), columns] = w
        new_1[rows_of(r), columns] = one
        new_2[rows_of(r), columns] = two
        return w.astype(bf16)

    to_heads = []

    def own_part(u, r, es):
        for d in range(1, nz):
            arrive(zb.at[z_from[d], es, rows_of(r)], zs.at[u, d - 1], zq.at[u, d - 1])
        total = zb[0, es, rows_of(r)].astype(f32)
        for i in range(1, nz):
            total += zb[i, es, rows_of(r)].astype(f32)
        low = part(x, r)
        rounded = total.astype(bf16)
        gf[low, es, rows_of(r)] = rounded
        for i in range(SPAN):
            e = es.start + i
            h = low + nx * e
            wb[e, rows_of(r)] = update(r, h, rounded[i].astype(f32))
            for d in x_order:
                copy = remote(
                    wb.at[e, rows_of(r)], wf.at[t, rows_of(r)],
                    ys.at[r, e, d], yq.at[r, lax.div(t, nx), d], (x_to[d], f, h),
                )
                if d > 0:
                    copy.start()
                    started.append(copy)
                else:
                    pl.when(h != t)(copy.start)
                    to_heads.append((h != t, copy))

            @pl.when(h == t)
            def _():
                wf[t, rows_of(r)] = wb[e, rows_of(r)]

    def collect(r):
        for e in range(hx):
            for d in range(nx):
                source = part(x_from[d], r) + nx * e
                piece = wf.at[source, rows_of(r)]
                wait = remote(piece, piece, ys.at[r, e, d], yq.at[r, e, d], (group, f, t)).wait_recv
                if d > 0:
                    wait()
                else:
                    pl.when(source != t)(wait)

    def gather_x(u, r, es):
        piece = gf.at[part(x, r), es, rows_of(r)]
        for d in range(1, nx):
            send(piece, piece, gs.at[u, d - 1], gq.at[u, d - 1], (x_to[d], f, t))

    def other_parts(u, r, es):
        for d in range(1, nx):
            low = part(x_from[d], r)
            arrive(gf.at[low, es, rows_of(r)], gs.at[u, d - 1], gq.at[u, d - 1])
            for i in range(SPAN):
                e = es.start + i
                update(r, low + nx * e, gf[low, e, rows_of(r)].astype(f32))

    x_order = sorted(range(nx), key=lambda d: -min(d, nx - d))

    def lay_out_tokens():
        others[0].wait()
        for i in range(nf):
            for row in range(tok_v.shape[0]):
                row_v[pl.ds(row * STEPS, STEPS)] = tok_v[row, :, pl.ds(i * depth, depth)].astype(f32)
            tb[i] = row_v[...].astype(bf16)
        tall[f] = tb[f]

    def attend_cache():
        for load in others[1:5]:
            load.wait()
        heads = QH // KVH
        qf[:, pl.ds(heads * STEPS, 4)] = jnp.zeros((qf.shape[0], 4, HD), f32)
        for head in range(heads):
            qf[:, pl.ds(head * STEPS, STEPS)] = q_v[:, :, pl.ds(head * HD, HD)].astype(f32)
        pad = qf.shape[1]
        query_rows[...] = qf[...].reshape(-1, HD).astype(bf16)
        slots = lax.broadcasted_iota(jnp.int32, (pad, k_v.shape[1]), 1)
        for row in range(qf.shape[0]):
            scores = lax.dot_general(
                qf[row].astype(bf16), k_v[row], (((1,), (1,)), ((), ())),
                preferred_element_type=f32,
            ) * SCORE_SCALE
            scores = jnp.where(slots < len_s[row], scores, masked_score)
            highest = jnp.max(scores, axis=-1, keepdims=True)
            exponent = jnp.exp(scores - highest)
            out = pl.ds(row * pad, pad)
            top[out] = jnp.broadcast_to(highest, (pad, HD))
            mass[out] = jnp.broadcast_to(jnp.sum(exponent, axis=-1, keepdims=True), (pad, HD))
            cached[out] = jnp.dot(exponent.astype(bf16), v_v[row], preferred_element_type=f32)
        token_rows = qf.shape[0] * STEPS
        at = lax.broadcasted_iota(jnp.int32, (token_rows, HD), 0)
        lane = lax.broadcasted_iota(jnp.int32, (token_rows, HD), 1)
        position = lax.rem(at, STEPS)
        for row in range(qf.shape[0]):
            position += jnp.where(lax.div(at, STEPS) == row, len_s[row], 0)
        power = lax.rem(lane, HD // 2).astype(f32) * (-2.0 / HD)
        angle = position.astype(f32) * jnp.exp(power * math.log(1000000.0))
        cosine[...] = jnp.cos(angle)
        turn = jnp.sin(angle)
        sine[...] = jnp.where(lane < HD // 2, -turn, turn)

    spans = range(0, hx, SPAN)
    units = [
        (r * len(spans) + i, r, pl.ds(e, SPAN)) for r in range(chunks) for i, e in enumerate(spans)
    ]
    per_chunk = len(spans)
    cast(0)
    pl.semaphore_wait(barrier, len(peers))
    for r in range(chunks):
        if r > 0:
            cast(r)
        for unit in units[r * per_chunk : (r + 1) * per_chunk]:
            scatter_x(*unit)
    for load in others:
        load.start()
    for unit in units:
        exchange_z(*unit)
    lay_out_tokens()
    f_order = sorted(range(1, nf), key=lambda k: -(k // 2))
    for k in f_order:
        send(tb.at[f_by[k]], tall.at[f], ts.at[k - 1], tq.at[k - 1], (group, f_by[k], t))
    for load in others[5:]:
        load.wait()
    for unit in units:
        own_part(*unit)
    for unit in units:
        gather_x(*unit)

    for k in f_order:
        arrive(tall.at[f_by[k]], ts.at[k - 1], tq.at[k - 1])
    for r in range(chunks):
        collect(r)
    partial = jnp.dot(
        tall[...].reshape(-1, depth), wf[...].reshape(depth, hc), preferred_element_type=f32
    ).reshape(pf.shape)
    pb[...] = partial.astype(bf16)
    for k in f_order:
        send(pb.at[f_by[k]], pr.at[f], ps.at[k - 1], pq.at[k - 1], (group, f_by[k], t))
    pf[...] = partial
    attend_cache()
    for unit in units:
        other_parts(*unit)
    total = pf[f]
    for k in f_order:
        arrive(pr.at[f_by[k]], ps.at[k - 1], pq.at[k - 1])
        total += pr[f_by[k]].astype(f32)
    projected[...] = total
    for copy in started:
        copy.wait_send()
    for apart, copy in to_heads:
        pl.when(apart)(copy.wait_send)


def finish_kernel(
    new_w, new_1, new_2, projected, query_rows, top, mass, cached, cosine, sine,
    w_out, m1_out, m2_out, kv_out, context_out, kv_v, context_v, merged, sem,
):
    f32 = jnp.float32
    bf16 = jnp.bfloat16
    stores = [
        pltpu.make_async_copy(src, dst, sem.at[i])
        for i, (src, dst) in enumerate(
            ((new_w, w_out), (new_1, m1_out), (new_2, m2_out), (kv_v, kv_out), (context_v, context_out))
        )
    ]
    for store in stores[:3]:
        store.start()
    rows = kv_v.shape[0]
    token_rows = projected.shape[0]
    pad = query_rows.shape[0] // rows
    keys = projected[:, :HD]
    keys = keys * cosine[...] + pltpu.roll(keys, HD // 2, 1) * sine[...]
    values = projected[:, HD:]
    for row in range(rows):
        span = slice(row * STEPS, (row + 1) * STEPS)
        kv_v[row, :, :HD] = keys[span].astype(bf16)
        kv_v[row, :, HD:] = values[span].astype(bf16)
    stores[3].start()
    scores = lax.dot_general(
        query_rows[...], keys.astype(bf16), (((1,), (1,)), ((), ())), preferred_element_type=f32
    ) * SCORE_SCALE
    at = lax.broadcasted_iota(jnp.int32, scores.shape, 0)
    new = lax.broadcasted_iota(jnp.int32, scores.shape, 1)
    seen = (lax.div(at, pad) == lax.div(new, STEPS)) & (lax.rem(new, STEPS) <= lax.rem(at, STEPS))
    scores = jnp.where(seen, scores, masked_score)
    highest = jnp.maximum(jnp.max(scores, axis=-1, keepdims=True), top[...])
    exponent = jnp.exp(scores - highest[:, :token_rows])
    kept = jnp.exp(top[...] - highest)
    weight = kept * mass[...] + jnp.sum(exponent, axis=-1, keepdims=True)
    context = kept * cached[...] + jnp.dot(
        exponent.astype(bf16), values.astype(bf16), preferred_element_type=f32
    )
    merged[...] = (context / weight).reshape(merged.shape)
    for head in range(QH // KVH):
        context_v[:, :, pl.ds(head * HD, HD)] = merged[:, pl.ds(head * STEPS, STEPS)].astype(bf16)
    stores[4].start()
    for store in stores:
        store.wait()


def shards(
    sizes, tokens, queries, cache_keys, cache_values, lengths, weights, moment1, moment2, grad_parts
):
    nx, nz, nf, nt = sizes
    rows, columns = weights.shape
    row_count = tokens.shape[0]
    token_rows = row_count * STEPS
    span = cache_keys.shape[1]
    hx = nt // nx
    hc = columns // nt
    depth = nt * rows
    chunks = rows // CHUNK
    pad = 8 * pl.cdiv(STEPS * (QH // KVH), 8)
    dma = pltpu.SemaphoreType.DMA
    f32 = jnp.float32
    bf16 = jnp.bfloat16
    hbm = pl.BlockSpec(memory_space=pltpu.HBM)
    vmem = pl.BlockSpec(memory_space=pltpu.VMEM)
    shape = jax.ShapeDtypeStruct
    block = shape((rows, columns), f32)
    held = pl.pallas_call(
        functools.partial(exchange_kernel, nx, nz, nf, nt),
        out_shape=[block] * 3
        + [shape((token_rows, hc), f32), shape((row_count * pad, HD), bf16)]
        + [shape((row_count * pad, HD), f32)] * 3
        + [shape((token_rows, HD), f32)] * 2,
        in_specs=[hbm] * 9,
        out_specs=[vmem] * 10,
        scratch_shapes=[pltpu.VMEM((rows, columns), f32)] * 4
        + [
            pltpu.VMEM(tokens.shape, bf16),
            pltpu.VMEM(queries.shape, bf16),
            pltpu.VMEM(cache_keys.shape, bf16),
            pltpu.VMEM(cache_values.shape, bf16),
            pltpu.SMEM(lengths.shape, jnp.int32),
            pltpu.VMEM((token_rows, depth), f32),
            pltpu.VMEM((nf, token_rows, depth), bf16),
            pltpu.VMEM((row_count, pad, HD), f32),
            pltpu.VMEM((nx, hx, rows, hc), bf16),
            pltpu.VMEM((nx - 1, hx, rows, hc), bf16),
            pltpu.VMEM((nz, hx, rows, hc), bf16),
            pltpu.VMEM((nx, hx, rows, hc), bf16),
            pltpu.VMEM((hx, rows, hc), bf16),
            pltpu.VMEM((nt, rows, hc), bf16),
            pltpu.VMEM((nf, token_rows, depth), bf16),
            pltpu.VMEM((nf, token_rows, hc), f32),
            pltpu.VMEM((nf, token_rows, hc), bf16),
            pltpu.VMEM((nf, token_rows, hc), bf16),
            dma((chunks,)),
            dma((8,)),
        ]
        + [dma((chunks * hx // SPAN, nx - 1))] * 2
        + [dma((chunks * hx // SPAN, nz - 1))] * 2
        + [dma((chunks * hx // SPAN, nx - 1))] * 2
        + [dma((chunks, hx, nx))] * 2
        + [dma((nf - 1,))] * 4,
        compiler_params=pltpu.CompilerParams(
            collective_id=0, has_side_effects=True, vmem_limit_bytes=40 << 20
        ),
        name="exchange",
    )(
        *(
            pltpu.with_memory_space_constraint(operand, pltpu.HBM)
            for operand in (
                grad_parts, weights, moment1, moment2, tokens, queries, cache_keys, cache_values, lengths
            )
        )
    )
    return pl.pallas_call(
        finish_kernel,
        out_shape=[block] * 3
        + [shape((row_count, STEPS, hc), bf16), shape(queries.shape, bf16)],
        in_specs=[vmem] * 10,
        out_specs=[hbm] * 5,
        scratch_shapes=[
            pltpu.VMEM((row_count, STEPS, hc), bf16),
            pltpu.VMEM(queries.shape, bf16),
            pltpu.VMEM((row_count, pad, HD), f32),
            dma((5,)),
        ],
        compiler_params=pltpu.CompilerParams(vmem_limit_bytes=16 << 20),
        name="finish",
    )(*held)


def solution(mesh):
    in_specs = (
        P(("group", "fsdp"), None, None),
        P(("group", "fsdp"), None, "tp"),
        P(("group", "fsdp"), None, "tp"),
        P(("group", "fsdp"), None, "tp"),
        P(("group", "fsdp")),
        P(("fsdp", "tp"), None),
        P(("fsdp", "tp"), None),
        P(("fsdp", "tp"), None),
        P("group", ("fsdp", "tp"), None),
    )
    out_specs = (
        P(("fsdp", "tp"), None),
        P(("fsdp", "tp"), None),
        P(("fsdp", "tp"), None),
        P(("group", "fsdp"), None, "tp"),
        P(("group", "fsdp"), None, "tp"),
    )
    nx = X_CHIPS
    sizes = (nx, mesh.shape["group"] // nx, mesh.shape["fsdp"], mesh.shape["tp"])
    return jax.shard_map(
        functools.partial(shards, sizes),
        mesh=mesh,
        in_specs=in_specs,
        out_specs=out_specs,
        check_vma=False,
    )
```

```python
import functools
import math

import jax
import jax.numpy as jnp
from jax import lax
from jax.experimental import pallas as pl
from jax.experimental.pallas import tpu as pltpu
from jax.sharding import PartitionSpec as P

QH = 40
KVH = 8
HD = 128
STEPS = 4
X_CHIPS = 4
SPAN = 1
CHUNK = 16

beta_one = 0.9
beta_two = 0.95
learning_rate = 0.004
decay_rate = 0.1
epsilon = 1e-08
correct_one = 1.0 - 0.9**10
correct_two = 1.0 - 0.95**10
masked_score = -1e30
SCORE_SCALE = 1.0 / math.sqrt(HD)

MESH = pl.DeviceIdType.MESH


def adam_update(weights, moment1, moment2, gradient):
    new_moment1 = beta_one * moment1 + (1.0 - beta_one) * gradient
    new_moment2 = beta_two * moment2 + (1.0 - beta_two) * gradient * gradient
    direction = new_moment1 * (1.0 / correct_one) / (jnp.sqrt(new_moment2 * (1.0 / correct_two)) + epsilon)
    new_weights = weights - learning_rate * (direction + decay_rate * weights)
    return (new_weights, new_moment1, new_moment2)


def flip(value, bits):
    out = value
    for b in range(bits.bit_length()):
        if (bits >> b) % 2:
            out = out + (1 << b) * (1 - 2 * lax.rem(lax.div(value, 1 << b), 2))
    return out


def exchange_kernel(
    nx, nz, nf, nt,
    grad, weights, moment1, moment2, tokens, queries, cache_keys, cache_values, lengths,
    new_w, new_1, new_2, projected, query_rows, top, mass, cached, cosine, sine,
    grad_v, w_v, m1_v, m2_v, tok_v, q_v, k_v, v_v, len_s, row_v, tb, qf,
    gb, xr, zb, gf, wb, wf, tall, pf, pb, pr,
    grad_sem, in_sem, xs, xq, zs, zq, gs, gq, ys, yq, ts, tq, ps, pq,
):
    group = lax.axis_index("group")
    f = lax.axis_index("fsdp")
    t = lax.axis_index("tp")
    x = lax.rem(group, nx)
    z = lax.div(group, nx)
    rows_all = grad_v.shape[0]
    hc = wf.shape[2]
    hx = nt // nx
    depth = tall.shape[2]
    chunks = rows_all // CHUNK
    f32 = jnp.float32
    bf16 = jnp.bfloat16

    x_to = [z * nx + lax.rem(x + d, nx) for d in range(nx)]
    z_to = [lax.rem(z + d, nz) * nx + x for d in range(nz)]
    f_by = [flip(f, k) for k in range(nf)]
    t_at = [lax.rem(t + d, nt) for d in range(nt)]
    x_from = [lax.rem(x + nx - d, nx) for d in range(nx)]
    z_from = [lax.rem(z + nz - d, nz) for d in range(nz)]

    barrier = pltpu.get_barrier_semaphore()
    peers = (
        [(z_to[d], f, t) for d in range(1, nz)]
        + [(group, f, t_at[d]) for d in range(1, nt)]
        + [(group, f_by[k], t) for k in range(1, nf)]
        + [(x_to[d], f, t) for d in range(1, nx)]
    )
    for peer in peers:
        pl.semaphore_signal(barrier, inc=1, device_id=peer, device_id_type=MESH)

    def rows_of(r):
        return pl.ds(r * CHUNK, CHUNK)

    loads = [
        pltpu.make_async_copy(grad.at[0, rows_of(r)], grad_v.at[rows_of(r)], grad_sem.at[r])
        for r in range(chunks)
    ]
    others = [
        pltpu.make_async_copy(src, dst, in_sem.at[i])
        for i, (src, dst) in enumerate(
            (
                (tokens, tok_v), (queries, q_v), (lengths, len_s), (cache_keys, k_v),
                (cache_values, v_v), (weights, w_v), (moment1, m1_v), (moment2, m2_v),
            )
        )
    ]
    for load in loads:
        load.start()

    def cast(r):
        loads[r].wait()
        for h in range(nx * hx):
            gb[h % nx, h // nx, rows_of(r)] = grad_v[rows_of(r), pl.ds(h * hc, hc)].astype(bf16)

    def remote(src, dst, send, recv, device):
        return pltpu.make_async_remote_copy(
            src_ref=src, dst_ref=dst, send_sem=send, recv_sem=recv,
            device_id=device, device_id_type=MESH,
        )

    started = []

    def send(*args):
        copy = remote(*args)
        copy.start()
        started.append(copy)

    def arrive(dst, send_sem, recv_sem):
        remote(dst, dst, send_sem, recv_sem, (group, f, t)).wait_recv()

    def part(at_x, r):
        return lax.rem(at_x - r - t + nx * (chunks + nt), nx)

    def scatter_x(u, r, es):
        for d in range(1, nx):
            send(
                gb.at[part(lax.rem(x + d, nx), r), es, rows_of(r)], xr.at[d - 1, es, rows_of(r)],
                xs.at[u, d - 1], xq.at[u, d - 1], (x_to[d], f, t),
            )

    def exchange_z(u, r, es):
        total = gb[part(x, r), es, rows_of(r)].astype(f32)
        for d in range(1, nx):
            arrive(xr.at[d - 1, es, rows_of(r)], xs.at[u, d - 1], xq.at[u, d - 1])
            total += xr[d - 1, es, rows_of(r)].astype(f32)
        zb[z, es, rows_of(r)] = total.astype(bf16)
        piece = zb.at[z, es, rows_of(r)]
        for d in range(1, nz):
            send(piece, piece, zs.at[u, d - 1], zq.at[u, d - 1], (z_to[d], f, t))

    def update(r, h, gradient):
        columns = pl.ds(pl.multiple_of(h * hc, hc), hc)
        w, one, two = adam_update(
            w_v[rows_of(r), columns], m1_v[rows_of(r), columns], m2_v[rows_of(r), columns], gradient
        )
        new_w[rows_of(r), columns] = w
        new_1[rows_of(r), columns] = one
        new_2[rows_of(r), columns] = two
        return w.astype(bf16)

    to_heads = []

    def own_part(u, r, es):
        for d in range(1, nz):
            arrive(zb.at[z_from[d], es, rows_of(r)], zs.at[u, d - 1], zq.at[u, d - 1])
        total = zb[0, es, rows_of(r)].astype(f32)
        for i in range(1, nz):
            total += zb[i, es, rows_of(r)].astype(f32)
        low = part(x, r)
        rounded = total.astype(bf16)
        gf[low, es, rows_of(r)] = rounded
        for i in range(SPAN):
            e = es.start + i
            h = low + nx * e
            wb[e, rows_of(r)] = update(r, h, rounded[i].astype(f32))
            for d in x_order:
                copy = remote(
                    wb.at[e, rows_of(r)], wf.at[t, rows_of(r)],
                    ys.at[r, e, d], yq.at[r, lax.div(t, nx), d], (x_to[d], f, h),
                )
                if d > 0:
                    copy.start()
                    started.append(copy)
                else:
                    pl.when(h != t)(copy.start)
                    to_heads.append((h != t, copy))

            @pl.when(h == t)
            def _():
                wf[t, rows_of(r)] = wb[e, rows_of(r)]

    def collect(r):
        for e in range(hx):
            for d in range(nx):
                source = part(x_from[d], r) + nx * e
                piece = wf.at[source, rows_of(r)]
                wait = remote(piece, piece, ys.at[r, e, d], yq.at[r, e, d], (group, f, t)).wait_recv
                if d > 0:
                    wait()
                else:
                    pl.when(source != t)(wait)

    def gather_x(u, r, es):
        piece = gf.at[part(x, r), es, rows_of(r)]
        for d in range(1, nx):
            send(piece, piece, gs.at[u, d - 1], gq.at[u, d - 1], (x_to[d], f, t))

    def other_parts(u, r, es):
        for d in range(1, nx):
            low = part(x_from[d], r)
            arrive(gf.at[low, es, rows_of(r)], gs.at[u, d - 1], gq.at[u, d - 1])
            for i in range(SPAN):
                e = es.start + i
                update(r, low + nx * e, gf[low, e, rows_of(r)].astype(f32))

    x_order = sorted(range(nx), key=lambda d: -min(d, nx - d))

    def lay_out_tokens():
        others[0].wait()
        for i in range(nf):
            for row in range(tok_v.shape[0]):
                row_v[pl.ds(row * STEPS, STEPS)] = tok_v[row, :, pl.ds(i * depth, depth)].astype(f32)
            tb[i] = row_v[...].astype(bf16)
        tall[f] = tb[f]

    def attend_cache():
        for load in others[1:5]:
            load.wait()
        heads = QH // KVH
        qf[:, pl.ds(heads * STEPS, 4)] = jnp.zeros((qf.shape[0], 4, HD), f32)
        for head in range(heads):
            qf[:, pl.ds(head * STEPS, STEPS)] = q_v[:, :, pl.ds(head * HD, HD)].astype(f32)
        pad = qf.shape[1]
        query_rows[...] = qf[...].reshape(-1, HD).astype(bf16)
        slots = lax.broadcasted_iota(jnp.int32, (pad, k_v.shape[1]), 1)
        for row in range(qf.shape[0]):
            scores = lax.dot_general(
                qf[row].astype(bf16), k_v[row], (((1,), (1,)), ((), ())),
                preferred_element_type=f32,
            ) * SCORE_SCALE
            scores = jnp.where(slots < len_s[row], scores, masked_score)
            highest = jnp.max(scores, axis=-1, keepdims=True)
            exponent = jnp.exp(scores - highest)
            out = pl.ds(row * pad, pad)
            top[out] = jnp.broadcast_to(highest, (pad, HD))
            mass[out] = jnp.broadcast_to(jnp.sum(exponent, axis=-1, keepdims=True), (pad, HD))
            cached[out] = jnp.dot(exponent.astype(bf16), v_v[row], preferred_element_type=f32)
        token_rows = qf.shape[0] * STEPS
        at = lax.broadcasted_iota(jnp.int32, (token_rows, HD), 0)
        lane = lax.broadcasted_iota(jnp.int32, (token_rows, HD), 1)
        position = lax.rem(at, STEPS)
        for row in range(qf.shape[0]):
            position += jnp.where(lax.div(at, STEPS) == row, len_s[row], 0)
        power = lax.rem(lane, HD // 2).astype(f32) * (-2.0 / HD)
        angle = position.astype(f32) * jnp.exp(power * math.log(1000000.0))
        cosine[...] = jnp.cos(angle)
        turn = jnp.sin(angle)
        sine[...] = jnp.where(lane < HD // 2, -turn, turn)

    spans = range(0, hx, SPAN)
    units = [
        (r * len(spans) + i, r, pl.ds(e, SPAN)) for r in range(chunks) for i, e in enumerate(spans)
    ]
    per_chunk = len(spans)
    cast(0)
    pl.semaphore_wait(barrier, len(peers))
    for r in range(chunks):
        if r > 0:
            cast(r)
        for unit in units[r * per_chunk : (r + 1) * per_chunk]:
            scatter_x(*unit)
    for load in others:
        load.start()
    for unit in units:
        exchange_z(*unit)
    lay_out_tokens()
    f_order = sorted(range(1, nf), key=lambda k: -(k // 2))
    for load in others[5:]:
        load.wait()
    for unit in units[:4]:
        own_part(*unit)
    for k in f_order:
        send(tb.at[f_by[k]], tall.at[f], ts.at[k - 1], tq.at[k - 1], (group, f_by[k], t))
    for unit in units[4:]:
        own_part(*unit)
    for unit in units:
        gather_x(*unit)

    for k in f_order:
        arrive(tall.at[f_by[k]], ts.at[k - 1], tq.at[k - 1])
    for r in range(chunks):
        collect(r)
    partial = jnp.dot(
        tall[...].reshape(-1, depth), wf[...].reshape(depth, hc), preferred_element_type=f32
    ).reshape(pf.shape)
    pb[...] = partial.astype(bf16)
    for k in f_order:
        send(pb.at[f_by[k]], pr.at[f], ps.at[k - 1], pq.at[k - 1], (group, f_by[k], t))
    pf[...] = partial
    attend_cache()
    for unit in units:
        other_parts(*unit)
    total = pf[f]
    for k in f_order:
        arrive(pr.at[f_by[k]], ps.at[k - 1], pq.at[k - 1])
        total += pr[f_by[k]].astype(f32)
    projected[...] = total
    for copy in started:
        copy.wait_send()
    for apart, copy in to_heads:
        pl.when(apart)(copy.wait_send)


def finish_kernel(
    new_w, new_1, new_2, projected, query_rows, top, mass, cached, cosine, sine,
    w_out, m1_out, m2_out, kv_out, context_out, kv_v, context_v, merged, sem,
):
    f32 = jnp.float32
    bf16 = jnp.bfloat16
    stores = [
        pltpu.make_async_copy(src, dst, sem.at[i])
        for i, (src, dst) in enumerate(
            ((new_w, w_out), (new_1, m1_out), (new_2, m2_out), (kv_v, kv_out), (context_v, context_out))
        )
    ]
    for store in stores[:3]:
        store.start()
    rows = kv_v.shape[0]
    token_rows = projected.shape[0]
    pad = query_rows.shape[0] // rows
    keys = projected[:, :HD]
    keys = keys * cosine[...] + pltpu.roll(keys, HD // 2, 1) * sine[...]
    values = projected[:, HD:]
    for row in range(rows):
        span = slice(row * STEPS, (row + 1) * STEPS)
        kv_v[row, :, :HD] = keys[span].astype(bf16)
        kv_v[row, :, HD:] = values[span].astype(bf16)
    stores[3].start()
    scores = lax.dot_general(
        query_rows[...], keys.astype(bf16), (((1,), (1,)), ((), ())), preferred_element_type=f32
    ) * SCORE_SCALE
    at = lax.broadcasted_iota(jnp.int32, scores.shape, 0)
    new = lax.broadcasted_iota(jnp.int32, scores.shape, 1)
    seen = (lax.div(at, pad) == lax.div(new, STEPS)) & (lax.rem(new, STEPS) <= lax.rem(at, STEPS))
    scores = jnp.where(seen, scores, masked_score)
    highest = jnp.maximum(jnp.max(scores, axis=-1, keepdims=True), top[...])
    exponent = jnp.exp(scores - highest[:, :token_rows])
    kept = jnp.exp(top[...] - highest)
    weight = kept * mass[...] + jnp.sum(exponent, axis=-1, keepdims=True)
    context = kept * cached[...] + jnp.dot(
        exponent.astype(bf16), values.astype(bf16), preferred_element_type=f32
    )
    merged[...] = (context / weight).reshape(merged.shape)
    for head in range(QH // KVH):
        context_v[:, :, pl.ds(head * HD, HD)] = merged[:, pl.ds(head * STEPS, STEPS)].astype(bf16)
    stores[4].start()
    for store in stores:
        store.wait()


def shards(
    sizes, tokens, queries, cache_keys, cache_values, lengths, weights, moment1, moment2, grad_parts
):
    nx, nz, nf, nt = sizes
    rows, columns = weights.shape
    row_count = tokens.shape[0]
    token_rows = row_count * STEPS
    span = cache_keys.shape[1]
    hx = nt // nx
    hc = columns // nt
    depth = nt * rows
    chunks = rows // CHUNK
    pad = 8 * pl.cdiv(STEPS * (QH // KVH), 8)
    dma = pltpu.SemaphoreType.DMA
    f32 = jnp.float32
    bf16 = jnp.bfloat16
    hbm = pl.BlockSpec(memory_space=pltpu.HBM)
    vmem = pl.BlockSpec(memory_space=pltpu.VMEM)
    shape = jax.ShapeDtypeStruct
    block = shape((rows, columns), f32)
    held = pl.pallas_call(
        functools.partial(exchange_kernel, nx, nz, nf, nt),
        out_shape=[block] * 3
        + [shape((token_rows, hc), f32), shape((row_count * pad, HD), bf16)]
        + [shape((row_count * pad, HD), f32)] * 3
        + [shape((token_rows, HD), f32)] * 2,
        in_specs=[hbm] * 9,
        out_specs=[vmem] * 10,
        scratch_shapes=[pltpu.VMEM((rows, columns), f32)] * 4
        + [
            pltpu.VMEM(tokens.shape, bf16),
            pltpu.VMEM(queries.shape, bf16),
            pltpu.VMEM(cache_keys.shape, bf16),
            pltpu.VMEM(cache_values.shape, bf16),
            pltpu.SMEM(lengths.shape, jnp.int32),
            pltpu.VMEM((token_rows, depth), f32),
            pltpu.VMEM((nf, token_rows, depth), bf16),
            pltpu.VMEM((row_count, pad, HD), f32),
            pltpu.VMEM((nx, hx, rows, hc), bf16),
            pltpu.VMEM((nx - 1, hx, rows, hc), bf16),
            pltpu.VMEM((nz, hx, rows, hc), bf16),
            pltpu.VMEM((nx, hx, rows, hc), bf16),
            pltpu.VMEM((hx, rows, hc), bf16),
            pltpu.VMEM((nt, rows, hc), bf16),
            pltpu.VMEM((nf, token_rows, depth), bf16),
            pltpu.VMEM((nf, token_rows, hc), f32),
            pltpu.VMEM((nf, token_rows, hc), bf16),
            pltpu.VMEM((nf, token_rows, hc), bf16),
            dma((chunks,)),
            dma((8,)),
        ]
        + [dma((chunks * hx // SPAN, nx - 1))] * 2
        + [dma((chunks * hx // SPAN, nz - 1))] * 2
        + [dma((chunks * hx // SPAN, nx - 1))] * 2
        + [dma((chunks, hx, nx))] * 2
        + [dma((nf - 1,))] * 4,
        compiler_params=pltpu.CompilerParams(
            collective_id=0, has_side_effects=True, vmem_limit_bytes=40 << 20
        ),
        name="exchange",
    )(
        *(
            pltpu.with_memory_space_constraint(operand, pltpu.HBM)
            for operand in (
                grad_parts, weights, moment1, moment2, tokens, queries, cache_keys, cache_values, lengths
            )
        )
    )
    return pl.pallas_call(
        finish_kernel,
        out_shape=[block] * 3
        + [shape((row_count, STEPS, hc), bf16), shape(queries.shape, bf16)],
        in_specs=[vmem] * 10,
        out_specs=[hbm] * 5,
        scratch_shapes=[
            pltpu.VMEM((row_count, STEPS, hc), bf16),
            pltpu.VMEM(queries.shape, bf16),
            pltpu.VMEM((row_count, pad, HD), f32),
            dma((5,)),
        ],
        compiler_params=pltpu.CompilerParams(vmem_limit_bytes=16 << 20),
        name="finish",
    )(*held)


def solution(mesh):
    in_specs = (
        P(("group", "fsdp"), None, None),
        P(("group", "fsdp"), None, "tp"),
        P(("group", "fsdp"), None, "tp"),
        P(("group", "fsdp"), None, "tp"),
        P(("group", "fsdp")),
        P(("fsdp", "tp"), None),
        P(("fsdp", "tp"), None),
        P(("fsdp", "tp"), None),
        P("group", ("fsdp", "tp"), None),
    )
    out_specs = (
        P(("fsdp", "tp"), None),
        P(("fsdp", "tp"), None),
        P(("fsdp", "tp"), None),
        P(("group", "fsdp"), None, "tp"),
        P(("group", "fsdp"), None, "tp"),
    )
    nx = X_CHIPS
    sizes = (nx, mesh.shape["group"] // nx, mesh.shape["fsdp"], mesh.shape["tp"])
    return jax.shard_map(
        functools.partial(shards, sizes),
        mesh=mesh,
        in_specs=in_specs,
        out_specs=out_specs,
        check_vma=False,
    )
```

```python
import functools
import math

import jax
import jax.numpy as jnp
from jax import lax
from jax.experimental import pallas as pl
from jax.experimental.pallas import tpu as pltpu
from jax.sharding import PartitionSpec as P

QH = 40
KVH = 8
HD = 128
STEPS = 4
X_CHIPS = 4
SPAN = 1
CHUNK = 16

beta_one = 0.9
beta_two = 0.95
learning_rate = 0.004
decay_rate = 0.1
epsilon = 1e-08
correct_one = 1.0 - 0.9**10
correct_two = 1.0 - 0.95**10
masked_score = -1e30
SCORE_SCALE = 1.0 / math.sqrt(HD)

MESH = pl.DeviceIdType.MESH


def adam_update(weights, moment1, moment2, gradient):
    new_moment1 = beta_one * moment1 + (1.0 - beta_one) * gradient
    new_moment2 = beta_two * moment2 + (1.0 - beta_two) * gradient * gradient
    direction = new_moment1 * (1.0 / correct_one) / (jnp.sqrt(new_moment2 * (1.0 / correct_two)) + epsilon)
    new_weights = weights - learning_rate * (direction + decay_rate * weights)
    return (new_weights, new_moment1, new_moment2)


def flip(value, bits):
    out = value
    for b in range(bits.bit_length()):
        if (bits >> b) % 2:
            out = out + (1 << b) * (1 - 2 * lax.rem(lax.div(value, 1 << b), 2))
    return out


def exchange_kernel(
    nx, nz, nf, nt,
    grad, weights, moment1, moment2, tokens, queries, cache_keys, cache_values, lengths,
    new_w, new_1, new_2, projected, query_rows, top, mass, cached, cosine, sine,
    grad_v, w_v, m1_v, m2_v, tok_v, q_v, k_v, v_v, len_s, row_v, tb, qf,
    gb, xr, zb, gf, wb, wf, tall, pf, pb, pr,
    go_z, go_t, go_f, grad_sem, in_sem, xs, xq, zs, zq, gs, gq, ys, yq, ts, tq, ps, pq,
):
    group = lax.axis_index("group")
    f = lax.axis_index("fsdp")
    t = lax.axis_index("tp")
    x = lax.rem(group, nx)
    z = lax.div(group, nx)
    rows_all = grad_v.shape[0]
    hc = wf.shape[2]
    hx = nt // nx
    depth = tall.shape[2]
    chunks = rows_all // CHUNK
    f32 = jnp.float32
    bf16 = jnp.bfloat16

    x_to = [z * nx + lax.rem(x + d, nx) for d in range(nx)]
    z_to = [lax.rem(z + d, nz) * nx + x for d in range(nz)]
    f_by = [flip(f, k) for k in range(nf)]
    t_at = [lax.rem(t + d, nt) for d in range(nt)]
    x_from = [lax.rem(x + nx - d, nx) for d in range(nx)]
    z_from = [lax.rem(z + nz - d, nz) for d in range(nz)]

    def place(at_t):
        return jnp.where(at_t > nt // 2, 2 * (nt - at_t), jnp.maximum(2 * at_t - 1, 0))

    rank = place(t)
    peers = (
        [((z_to[d], f, t), z + d < nz, go_z.at[nz - d - 1]) for d in range(1, nz)]
        + [((group, f, t_at[d]), place(t_at[d]) > rank, go_t) for d in range(1, nt)]
        + [((group, f_by[k], t), f_by[k] > f, go_f) for k in range(1, nf)]
    )
    barrier = pltpu.get_barrier_semaphore()

    def greet(semaphore, device):
        pl.semaphore_signal(semaphore, inc=1, device_id=device, device_id_type=MESH)

    for d in range(1, nx):
        greet(barrier, (x_to[d], f, t))
    for device, later, _ in peers:
        pl.when(later)(functools.partial(greet, barrier, device))

    def answer():
        pl.semaphore_wait(barrier, nx - 1 + z + rank + f)
        for device, later, go in peers:
            pl.when(jnp.logical_not(later))(functools.partial(greet, go, device))

    def rows_of(r):
        return pl.ds(r * CHUNK, CHUNK)

    loads = [
        pltpu.make_async_copy(grad.at[0, rows_of(r)], grad_v.at[rows_of(r)], grad_sem.at[r])
        for r in range(chunks)
    ]
    others = [
        pltpu.make_async_copy(src, dst, in_sem.at[i])
        for i, (src, dst) in enumerate(
            (
                (tokens, tok_v), (queries, q_v), (lengths, len_s), (cache_keys, k_v),
                (cache_values, v_v), (weights, w_v), (moment1, m1_v), (moment2, m2_v),
            )
        )
    ]
    for load in loads:
        load.start()

    def cast(r):
        loads[r].wait()
        for h in range(nx * hx):
            gb[h % nx, h // nx, rows_of(r)] = grad_v[rows_of(r), pl.ds(h * hc, hc)].astype(bf16)

    def remote(src, dst, send, recv, device):
        return pltpu.make_async_remote_copy(
            src_ref=src, dst_ref=dst, send_sem=send, recv_sem=recv,
            device_id=device, device_id_type=MESH,
        )

    started = []

    def send(*args):
        copy = remote(*args)
        copy.start()
        started.append(copy)

    def arrive(dst, send_sem, recv_sem):
        remote(dst, dst, send_sem, recv_sem, (group, f, t)).wait_recv()

    def part(at_x, r):
        return lax.rem(at_x - r - t + nx * (chunks + nt), nx)

    def scatter_x(u, r, es):
        for d in range(1, nx):
            send(
                gb.at[part(lax.rem(x + d, nx), r), es, rows_of(r)], xr.at[d - 1, es, rows_of(r)],
                xs.at[u, d - 1], xq.at[u, d - 1], (x_to[d], f, t),
            )

    def exchange_z(u, r, es):
        total = gb[part(x, r), es, rows_of(r)].astype(f32)
        for d in range(1, nx):
            arrive(xr.at[d - 1, es, rows_of(r)], xs.at[u, d - 1], xq.at[u, d - 1])
            total += xr[d - 1, es, rows_of(r)].astype(f32)
        zb[z, es, rows_of(r)] = total.astype(bf16)
        for d in range(1, nz):
            pl.when(z + d >= nz)(z_copy(d, u, r, es).start)

    def z_copy(d, u, r, es):
        piece = zb.at[z, es, rows_of(r)]
        return remote(piece, piece, zs.at[u, d - 1], zq.at[u, d - 1], (z_to[d], f, t))

    def exchange_z_later(d):
        @pl.when(z + d < nz)
        def _():
            pl.semaphore_wait(go_z.at[d - 1], 1)
            for unit in units:
                z_copy(d, *unit).start()

    def update(r, h, gradient):
        columns = pl.ds(pl.multiple_of(h * hc, hc), hc)
        w, one, two = adam_update(
            w_v[rows_of(r), columns], m1_v[rows_of(r), columns], m2_v[rows_of(r), columns], gradient
        )
        new_w[rows_of(r), columns] = w
        new_1[rows_of(r), columns] = one
        new_2[rows_of(r), columns] = two
        return w.astype(bf16)

    to_heads = []

    def own_part(u, r, es):
        for d in range(1, nz):
            arrive(zb.at[z_from[d], es, rows_of(r)], zs.at[u, d - 1], zq.at[u, d - 1])
        total = zb[0, es, rows_of(r)].astype(f32)
        for i in range(1, nz):
            total += zb[i, es, rows_of(r)].astype(f32)
        low = part(x, r)
        rounded = total.astype(bf16)
        gf[low, es, rows_of(r)] = rounded
        for i in range(SPAN):
            e = es.start + i
            h = low + nx * e
            wb[e, rows_of(r)] = update(r, h, rounded[i].astype(f32))
            for d in x_order:
                copy = remote(
                    wb.at[e, rows_of(r)], wf.at[t, rows_of(r)],
                    ys.at[r, e, d], yq.at[r, lax.div(t, nx), d], (x_to[d], f, h),
                )
                if d > 0:
                    copy.start()
                    started.append(copy)
                else:
                    pl.when(h != t)(copy.start)
                    to_heads.append((h != t, copy))

            @pl.when(h == t)
            def _():
                wf[t, rows_of(r)] = wb[e, rows_of(r)]

    def collect(r):
        for e in range(hx):
            for d in range(nx):
                source = part(x_from[d], r) + nx * e
                piece = wf.at[source, rows_of(r)]
                wait = remote(piece, piece, ys.at[r, e, d], yq.at[r, e, d], (group, f, t)).wait_recv
                if d > 0:
                    wait()
                else:
                    pl.when(source != t)(wait)

    def gather_x(u, r, es):
        piece = gf.at[part(x, r), es, rows_of(r)]
        for d in range(1, nx):
            send(piece, piece, gs.at[u, d - 1], gq.at[u, d - 1], (x_to[d], f, t))

    def other_parts(u, r, es):
        for d in range(1, nx):
            low = part(x_from[d], r)
            arrive(gf.at[low, es, rows_of(r)], gs.at[u, d - 1], gq.at[u, d - 1])
            for i in range(SPAN):
                e = es.start + i
                update(r, low + nx * e, gf[low, e, rows_of(r)].astype(f32))

    x_order = sorted(range(nx), key=lambda d: -min(d, nx - d))

    def lay_out_tokens():
        others[0].wait()
        for i in range(nf):
            for row in range(tok_v.shape[0]):
                row_v[pl.ds(row * STEPS, STEPS)] = tok_v[row, :, pl.ds(i * depth, depth)].astype(f32)
            tb[i] = row_v[...].astype(bf16)
        tall[f] = tb[f]

    def attend_cache():
        for load in others[1:5]:
            load.wait()
        heads = QH // KVH
        qf[:, pl.ds(heads * STEPS, 4)] = jnp.zeros((qf.shape[0], 4, HD), f32)
        for head in range(heads):
            qf[:, pl.ds(head * STEPS, STEPS)] = q_v[:, :, pl.ds(head * HD, HD)].astype(f32)
        pad = qf.shape[1]
        query_rows[...] = qf[...].reshape(-1, HD).astype(bf16)
        slots = lax.broadcasted_iota(jnp.int32, (pad, k_v.shape[1]), 1)
        for row in range(qf.shape[0]):
            scores = lax.dot_general(
                qf[row].astype(bf16), k_v[row], (((1,), (1,)), ((), ())),
                preferred_element_type=f32,
            ) * SCORE_SCALE
            scores = jnp.where(slots < len_s[row], scores, masked_score)
            highest = jnp.max(scores, axis=-1, keepdims=True)
            exponent = jnp.exp(scores - highest)
            out = pl.ds(row * pad, pad)
            top[out] = jnp.broadcast_to(highest, (pad, HD))
            mass[out] = jnp.broadcast_to(jnp.sum(exponent, axis=-1, keepdims=True), (pad, HD))
            cached[out] = jnp.dot(exponent.astype(bf16), v_v[row], preferred_element_type=f32)
        token_rows = qf.shape[0] * STEPS
        at = lax.broadcasted_iota(jnp.int32, (token_rows, HD), 0)
        lane = lax.broadcasted_iota(jnp.int32, (token_rows, HD), 1)
        position = lax.rem(at, STEPS)
        for row in range(qf.shape[0]):
            position += jnp.where(lax.div(at, STEPS) == row, len_s[row], 0)
        power = lax.rem(lane, HD // 2).astype(f32) * (-2.0 / HD)
        angle = position.astype(f32) * jnp.exp(power * math.log(1000000.0))
        cosine[...] = jnp.cos(angle)
        turn = jnp.sin(angle)
        sine[...] = jnp.where(lane < HD // 2, -turn, turn)

    spans = range(0, hx, SPAN)
    units = [
        (r * len(spans) + i, r, pl.ds(e, SPAN)) for r in range(chunks) for i, e in enumerate(spans)
    ]
    per_chunk = len(spans)
    cast(0)
    answer()
    for r in range(chunks):
        if r > 0:
            cast(r)
        for unit in units[r * per_chunk : (r + 1) * per_chunk]:
            scatter_x(*unit)
    for load in others:
        load.start()
    for unit in units:
        exchange_z(*unit)
    lay_out_tokens()

    @pl.when(f < nf - 1)
    def _():
        pl.semaphore_wait(go_f, nf - 1 - f)

    f_order = sorted(range(1, nf), key=lambda k: -(k // 2))
    for d in range(1, nz):
        exchange_z_later(d)
    for load in others[5:]:
        load.wait()

    @pl.when(rank < nt - 1)
    def _():
        pl.semaphore_wait(go_t, nt - 1 - rank)

    for unit in units[:4]:
        own_part(*unit)
    for k in f_order:
        send(tb.at[f_by[k]], tall.at[f], ts.at[k - 1], tq.at[k - 1], (group, f_by[k], t))
    for unit in units[4:]:
        own_part(*unit)
    for unit in units:
        gather_x(*unit)

    for k in f_order:
        arrive(tall.at[f_by[k]], ts.at[k - 1], tq.at[k - 1])
    for r in range(chunks):
        collect(r)
    partial = jnp.dot(
        tall[...].reshape(-1, depth), wf[...].reshape(depth, hc), preferred_element_type=f32
    ).reshape(pf.shape)
    pb[...] = partial.astype(bf16)
    for k in f_order:
        send(pb.at[f_by[k]], pr.at[f], ps.at[k - 1], pq.at[k - 1], (group, f_by[k], t))
    pf[...] = partial
    attend_cache()
    for unit in units:
        other_parts(*unit)
    total = pf[f]
    for k in f_order:
        arrive(pr.at[f_by[k]], ps.at[k - 1], pq.at[k - 1])
        total += pr[f_by[k]].astype(f32)
    projected[...] = total
    for copy in started:
        copy.wait_send()
    for d in range(1, nz):
        for unit in units:
            z_copy(d, *unit).wait_send()
    for apart, copy in to_heads:
        pl.when(apart)(copy.wait_send)


def finish_kernel(
    new_w, new_1, new_2, projected, query_rows, top, mass, cached, cosine, sine,
    w_out, m1_out, m2_out, kv_out, context_out, kv_v, context_v, merged, sem,
):
    f32 = jnp.float32
    bf16 = jnp.bfloat16
    stores = [
        pltpu.make_async_copy(src, dst, sem.at[i])
        for i, (src, dst) in enumerate(
            ((new_w, w_out), (new_1, m1_out), (new_2, m2_out), (kv_v, kv_out), (context_v, context_out))
        )
    ]
    for store in stores[:3]:
        store.start()
    rows = kv_v.shape[0]
    token_rows = projected.shape[0]
    pad = query_rows.shape[0] // rows
    keys = projected[:, :HD]
    keys = keys * cosine[...] + pltpu.roll(keys, HD // 2, 1) * sine[...]
    values = projected[:, HD:]
    for row in range(rows):
        span = slice(row * STEPS, (row + 1) * STEPS)
        kv_v[row, :, :HD] = keys[span].astype(bf16)
        kv_v[row, :, HD:] = values[span].astype(bf16)
    stores[3].start()
    scores = lax.dot_general(
        query_rows[...], keys.astype(bf16), (((1,), (1,)), ((), ())), preferred_element_type=f32
    ) * SCORE_SCALE
    at = lax.broadcasted_iota(jnp.int32, scores.shape, 0)
    new = lax.broadcasted_iota(jnp.int32, scores.shape, 1)
    seen = (lax.div(at, pad) == lax.div(new, STEPS)) & (lax.rem(new, STEPS) <= lax.rem(at, STEPS))
    scores = jnp.where(seen, scores, masked_score)
    highest = jnp.maximum(jnp.max(scores, axis=-1, keepdims=True), top[...])
    exponent = jnp.exp(scores - highest[:, :token_rows])
    kept = jnp.exp(top[...] - highest)
    weight = kept * mass[...] + jnp.sum(exponent, axis=-1, keepdims=True)
    context = kept * cached[...] + jnp.dot(
        exponent.astype(bf16), values.astype(bf16), preferred_element_type=f32
    )
    merged[...] = (context / weight).reshape(merged.shape)
    for head in range(QH // KVH):
        context_v[:, :, pl.ds(head * HD, HD)] = merged[:, pl.ds(head * STEPS, STEPS)].astype(bf16)
    stores[4].start()
    for store in stores:
        store.wait()


def shards(
    sizes, tokens, queries, cache_keys, cache_values, lengths, weights, moment1, moment2, grad_parts
):
    nx, nz, nf, nt = sizes
    rows, columns = weights.shape
    row_count = tokens.shape[0]
    token_rows = row_count * STEPS
    span = cache_keys.shape[1]
    hx = nt // nx
    hc = columns // nt
    depth = nt * rows
    chunks = rows // CHUNK
    pad = 8 * pl.cdiv(STEPS * (QH // KVH), 8)
    dma = pltpu.SemaphoreType.DMA
    f32 = jnp.float32
    bf16 = jnp.bfloat16
    hbm = pl.BlockSpec(memory_space=pltpu.HBM)
    vmem = pl.BlockSpec(memory_space=pltpu.VMEM)
    shape = jax.ShapeDtypeStruct
    block = shape((rows, columns), f32)
    held = pl.pallas_call(
        functools.partial(exchange_kernel, nx, nz, nf, nt),
        out_shape=[block] * 3
        + [shape((token_rows, hc), f32), shape((row_count * pad, HD), bf16)]
        + [shape((row_count * pad, HD), f32)] * 3
        + [shape((token_rows, HD), f32)] * 2,
        in_specs=[hbm] * 9,
        out_specs=[vmem] * 10,
        scratch_shapes=[pltpu.VMEM((rows, columns), f32)] * 4
        + [
            pltpu.VMEM(tokens.shape, bf16),
            pltpu.VMEM(queries.shape, bf16),
            pltpu.VMEM(cache_keys.shape, bf16),
            pltpu.VMEM(cache_values.shape, bf16),
            pltpu.SMEM(lengths.shape, jnp.int32),
            pltpu.VMEM((token_rows, depth), f32),
            pltpu.VMEM((nf, token_rows, depth), bf16),
            pltpu.VMEM((row_count, pad, HD), f32),
            pltpu.VMEM((nx, hx, rows, hc), bf16),
            pltpu.VMEM((nx - 1, hx, rows, hc), bf16),
            pltpu.VMEM((nz, hx, rows, hc), bf16),
            pltpu.VMEM((nx, hx, rows, hc), bf16),
            pltpu.VMEM((hx, rows, hc), bf16),
            pltpu.VMEM((nt, rows, hc), bf16),
            pltpu.VMEM((nf, token_rows, depth), bf16),
            pltpu.VMEM((nf, token_rows, hc), f32),
            pltpu.VMEM((nf, token_rows, hc), bf16),
            pltpu.VMEM((nf, token_rows, hc), bf16),
            pltpu.SemaphoreType.REGULAR((nz - 1,)),
            pltpu.SemaphoreType.REGULAR,
            pltpu.SemaphoreType.REGULAR,
            dma((chunks,)),
            dma((8,)),
        ]
        + [dma((chunks * hx // SPAN, nx - 1))] * 2
        + [dma((chunks * hx // SPAN, nz - 1))] * 2
        + [dma((chunks * hx // SPAN, nx - 1))] * 2
        + [dma((chunks, hx, nx))] * 2
        + [dma((nf - 1,))] * 4,
        compiler_params=pltpu.CompilerParams(
            collective_id=0, has_side_effects=True, vmem_limit_bytes=40 << 20
        ),
        name="exchange",
    )(
        *(
            pltpu.with_memory_space_constraint(operand, pltpu.HBM)
            for operand in (
                grad_parts, weights, moment1, moment2, tokens, queries, cache_keys, cache_values, lengths
            )
        )
    )
    return pl.pallas_call(
        finish_kernel,
        out_shape=[block] * 3
        + [shape((row_count, STEPS, hc), bf16), shape(queries.shape, bf16)],
        in_specs=[vmem] * 10,
        out_specs=[hbm] * 5,
        scratch_shapes=[
            pltpu.VMEM((row_count, STEPS, hc), bf16),
            pltpu.VMEM(queries.shape, bf16),
            pltpu.VMEM((row_count, pad, HD), f32),
            dma((5,)),
        ],
        compiler_params=pltpu.CompilerParams(vmem_limit_bytes=16 << 20),
        name="finish",
    )(*held)


def solution(mesh):
    in_specs = (
        P(("group", "fsdp"), None, None),
        P(("group", "fsdp"), None, "tp"),
        P(("group", "fsdp"), None, "tp"),
        P(("group", "fsdp"), None, "tp"),
        P(("group", "fsdp")),
        P(("fsdp", "tp"), None),
        P(("fsdp", "tp"), None),
        P(("fsdp", "tp"), None),
        P("group", ("fsdp", "tp"), None),
    )
    out_specs = (
        P(("fsdp", "tp"), None),
        P(("fsdp", "tp"), None),
        P(("fsdp", "tp"), None),
        P(("group", "fsdp"), None, "tp"),
        P(("group", "fsdp"), None, "tp"),
    )
    nx = X_CHIPS
    sizes = (nx, mesh.shape["group"] // nx, mesh.shape["fsdp"], mesh.shape["tp"])
    return jax.shard_map(
        functools.partial(shards, sizes),
        mesh=mesh,
        in_specs=in_specs,
        out_specs=out_specs,
        check_vma=False,
    )
```
